256 devices in a mesh: gx: 32 (over z, y_hi, core), gy: 2 (over y_lo), gz: 4 (over x).
Axes of the slice: x: 4, y: 4 (y_hi: 2, y_lo: 2; y = y_hi * 2 + y_lo), z: 8, core: 2. Of those that a mesh axis runs over, the one named last changes fastest.
Arguments:
- displacement: float32 [3, 256, 64, 256], P(None, 'gx', 'gz', 'gy'), may hold values from -0.75 to 0.75
- velocity: float32 [3, 256, 64, 256], P(None, 'gx', 'gz', 'gy'), may hold values from -1.5 to 1.5
- classes: int32 [256, 64, 256], P('gx', 'gz', 'gy'), may hold values from 0 to 3
- clamped: int32 [256, 64, 256], P('gx', 'gz', 'gy'), may hold values 0 or 1
- stiffness: float32 [4], replicated, may hold values from 1 to 8
- softening: float32 [4], replicated, may hold values from 0.03 to 0.3
Outputs:
- final_displacement: float32 [3, 256, 64, 256], P(None, 'gx', 'gz', 'gy')
- final_velocity: float32 [3, 256, 64, 256], P(None, 'gx', 'gz', 'gy')
The draws below stay inside these ranges and needn't reach their ends.
All inputs are finite; a program needn't handle non-finite values. No bound on the sum of `clamped` on one device may be relied on, other than what follows from the above.
Results may differ from the reference program's by a relative error of at most 0.000038.
Values sent between devices are 32-bit elements; how exact they have to be, the bound alone decides.
A program may use at most 64 MiB of HBM per device.

```python
import math
import jax
import jax.numpy as jnp

STEPS = 4
NCLASS = 4
NX = 256
NY = 256
NZ = 64


def place_ends(values, rng, least, largest):
    index_at = [jax.random.randint(jax.random.fold_in(rng, axis), (), 0, length) for axis, length in enumerate(values.shape)]
    widest = values.shape.index(max(values.shape))
    beside = index_at[:widest] + [(index_at[widest] + 1) % values.shape[widest]] + index_at[widest + 1:]
    return values.at[tuple(index_at)].set(least).at[tuple(beside)].set(largest)


def steps_of(rng, shape, cuts, smallest, high):
    loudness = 1.0
    for axis_at, blocks in cuts:
        draws = jax.random.uniform(jax.random.fold_in(jax.random.fold_in(rng, 6), axis_at), (blocks,), jnp.float32, smallest / len(cuts), high / len(cuts))
        loudness = loudness * jnp.repeat(jnp.exp(draws), shape[axis_at] // blocks).reshape((-1,) + (1,) * (len(shape) - 1 - axis_at))
    return loudness


def bell_draw(key, extent, width, most, cuts=(), kind=jnp.bfloat16):
    values = width * jax.random.normal(key, extent, jnp.float32)
    if cuts:
        values = values * steps_of(key, extent, cuts, -0.22, 0.18)
    return jnp.clip(values, -most, most).astype(kind)


def setup_inputs(seed: int = 0) -> dict:
    seeds = jax.random.split(jax.random.key(seed), 7)
    displacement = bell_draw(seeds[0], (3, NX, NZ, NY), 0.05, 0.75, ((1, 32), (2, 4), (3, 2)), jnp.float32)
    velocity = bell_draw(seeds[1], (3, NX, NZ, NY), 0.1, 1.5, ((1, 32), (2, 4), (3, 2)), jnp.float32)
    classes = place_ends(jax.random.randint(seeds[2], (NX, NZ, NY), 0, NCLASS), jax.random.fold_in(seeds[2], 1), 0, NCLASS - 1).astype(jnp.int32)
    clamped = place_ends((jax.random.randint(seeds[3], (NX, NZ, NY), 0, 8) < 1).astype(jnp.int32), jax.random.fold_in(seeds[3], 1), 0, 1)
    stiffness = jnp.clip(jnp.exp(jax.random.uniform(seeds[4], (NCLASS,), jnp.float32, math.log(1.0), math.log(8.0))), 1.0, 8.0)
    softening = jnp.clip(jnp.exp(jax.random.uniform(seeds[5], (NCLASS,), jnp.float32, math.log(0.03), math.log(0.3))), 0.03, 0.3)
    return dict(displacement=displacement, velocity=velocity, classes=classes, clamped=clamped, stiffness=stiffness, softening=softening)


bond_offsets = [(along_x, along_y, along_z) for along_x in range(-2, 3) for along_y in range(-2, 3) for along_z in range(-2, 3) if 0 < along_x * along_x + along_y * along_y + along_z * along_z <= 4]
time_step = 0.2

def bond_forces(padded, stiff_pad, soft_pad, valid_pad):
    size_x = padded.shape[1] - 4
    size_z = padded.shape[2] - 4
    size_y = padded.shape[3] - 4
    centre_part = padded[:, 2:-2, 2:-2, 2:-2]
    stiff_in = stiff_pad[2:-2, 2:-2, 2:-2]
    soft_in = soft_pad[2:-2, 2:-2, 2:-2]
    valid_in = valid_pad[2:-2, 2:-2, 2:-2]
    total_x = jnp.zeros(stiff_in.shape, jnp.float32)
    total_y = jnp.zeros(stiff_in.shape, jnp.float32)
    total_z = jnp.zeros(stiff_in.shape, jnp.float32)
    for along_x, along_y, along_z in bond_offsets:
        length = math.sqrt(along_x * along_x + along_y * along_y + along_z * along_z)
        window = (slice(2 + along_x, 2 + along_x + size_x), slice(2 + along_z, 2 + along_z + size_z), slice(2 + along_y, 2 + along_y + size_y))
        neighbour = padded[(slice(None),) + window]
        stretch_x = neighbour[0] - centre_part[0] + along_x
        stretch_y = neighbour[1] - centre_part[1] + along_y
        stretch_z = neighbour[2] - centre_part[2] + along_z
        distance = jnp.sqrt(stretch_x * stretch_x + stretch_y * stretch_y + stretch_z * stretch_z)
        strain = (distance - length) / length
        bond_stiff = 0.5 * (stiff_in + stiff_pad[window])
        bond_soft = 0.5 * (soft_in + soft_pad[window])
        tension = bond_stiff * strain * jnp.exp(-jnp.abs(strain) / bond_soft) * valid_pad[window] / (length * distance)
        total_x = total_x + tension * stretch_x
        total_y = total_y + tension * stretch_y
        total_z = total_z + tension * stretch_z
    return jnp.stack([total_x, total_y, total_z]) * valid_in

def reference(displacement, velocity, classes, clamped, stiffness, softening):
    stiff_pad = jnp.pad(stiffness[classes], 2)
    soft_pad = jnp.pad(softening[classes], 2, constant_values=1.0)
    valid_pad = jnp.pad(jnp.ones(classes.shape, jnp.float32), 2)
    free_node = 1.0 - clamped.astype(jnp.float32)
    widths = ((0, 0), (2, 2), (2, 2), (2, 2))
    acceleration = bond_forces(jnp.pad(displacement, widths), stiff_pad, soft_pad, valid_pad)
    moved_field = displacement
    velocity_now = velocity
    for step_index in range(STEPS):
        half_speed = free_node * (velocity_now + 0.5 * time_step * acceleration)
        moved_field = moved_field + time_step * half_speed
        acceleration = bond_forces(jnp.pad(moved_field, widths), stiff_pad, soft_pad, valid_pad)
        velocity_now = free_node * (half_speed + 0.5 * time_step * acceleration)
    return (moved_field, velocity_now)
```

```python
import math

import jax
import jax.numpy as jnp
from jax import lax
from jax.experimental import pallas as pl
from jax.experimental.pallas import tpu as pltpu
from jax.sharding import PartitionSpec as P

STEPS = 4
DT = 0.2
HALF = 0.1
MESH = pl.DeviceIdType.MESH

DIRS = [
    (ex, ey, ez)
    for ex in range(-2, 3)
    for ey in range(-2, 3)
    for ez in range(-2, 3)
    if 0 < ex * ex + ey * ey + ez * ez <= 4
]
WHERE = {e: n for n, e in enumerate(DIRS)}
PARTNERS = [
    (dx, dz, dy)
    for dx in (-1, 0, 1)
    for dz in (-1, 0, 1)
    for dy in (0, 1)
    if (dx, dz, dy) != (0, 0, 0)
]
SLOT = {d: n for n, d in enumerate(PARTNERS)}
NP = len(PARTNERS)
TINY = 1e-30


def opposite(d):
    return (-d[0], -d[1], d[2])


def kernel(
    table_c, table_q, u_in, v_in, class_in, clamp_in,
    u_out, v_out,
    grid, yp1, ym1, yp2, ym2, speed, cls, clm, free, acc, coef,
    zsend, zrecv, csend, crecv, qsend, qrecv,
    local_sem, send_sem, recv_sem,
):
    gx, gy, gz = lax.axis_index("gx"), lax.axis_index("gy"), lax.axis_index("gz")
    nx, nz = lax.axis_size("gx"), lax.axis_size("gz")

    def device(d):
        return {
            "gx": lax.rem(gx + (d[0] + nx), nx),
            "gz": lax.rem(gz + (d[1] + nz), nz),
            "gy": 1 - gy if d[2] else gy,
        }

    barrier = pltpu.get_barrier_semaphore()
    for d in PARTNERS:
        pl.semaphore_signal(barrier, inc=1, device_id=device(d), device_id_type=MESH)

    loads = [
        pltpu.make_async_copy(class_in, cls, local_sem.at[0]),
        pltpu.make_async_copy(u_in, grid.at[0, 0:3, 2:10, 8:24], local_sem.at[1]),
        pltpu.make_async_copy(v_in, speed, local_sem.at[2]),
        pltpu.make_async_copy(clamp_in, clm, local_sem.at[3]),
    ]
    for c in loads:
        c.start()

    lane = lax.broadcasted_iota(jnp.int32, (8, 128), 1)
    row = lax.broadcasted_iota(jnp.int32, (8, 128), 0)
    seam_from = jnp.where(gy == 1, 0, 126)
    pair = lax.rem(lane - seam_from + 128, 128) // 2
    lower = gy == 0

    seam = {
        1: (lane < 1) & lower,
        2: (lane < 2) & lower,
        -1: (lane > 126) & (gy == 1),
        -2: (lane > 125) & (gy == 1),
    }

    def transfers(s, nc, which=lambda d: True):
        out = []
        for d in PARTNERS:
            if not which(d):
                continue
            dx, dz, dy = d
            m = SLOT[d]
            o = SLOT[opposite(d)]
            if d == (-1, 0, 0):
                src, dst = grid.at[s, 0:nc, 2:4, 8:24], grid.at[s, 0:nc, 10:12, 8:24]
            elif d == (1, 0, 0):
                src, dst = grid.at[s, 0:nc, 8:10, 8:24], grid.at[s, 0:nc, 0:2, 8:24]
            elif dy == 0 and dx == 0:
                side = 0 if dz < 0 else 1
                src, dst = zsend.at[side, 0:nc], zrecv.at[s, 1 - side, 0:nc]
            elif dy == 0:
                q = (0 if dx < 0 else 2) + (0 if dz < 0 else 1)
                src, dst = csend.at[q], crecv.at[s, 3 - q]
            else:
                if dz == 0:
                    src, dst = qsend.at[...], qrecv.at[s, 1 - dx, 8:24]
                elif dz > 0:
                    src, dst = qsend.at[8:16], qrecv.at[s, 1 - dx, 0:8]
                else:
                    src, dst = qsend.at[0:8], qrecv.at[s, 1 - dx, 24:32]
            out.append(
                pltpu.make_async_remote_copy(
                    src_ref=src,
                    dst_ref=dst,
                    send_sem=send_sem.at[m],
                    recv_sem=recv_sem.at[s, o],
                    device_id=device(d),
                    device_id_type=MESH,
                )
            )
        return out

    def send_all(s, nc):
        for t in transfers(s, nc):
            t.start()

    def wait_sent(s, nc):
        for t in transfers(s, nc):
            t.wait_send()

    def wait_from(s, nc, which):
        for t in transfers(s, nc, which):
            t.wait_recv()

    def pack(s, planes, nc, fresh):
        for t in range(2):
            packed = None if fresh else qsend[8 * t : 8 * t + 8, :]
            for c in range(nc):
                for p in planes:
                    k = c * 8 + p
                    tile = grid[s, c, p + 2, 8 + 8 * t : 16 + 8 * t, :]
                    moved = pltpu.roll(tile, 2 * k, 1) if k else tile
                    packed = moved if packed is None else jnp.where(pair == k, moved, packed)
            qsend[8 * t : 8 * t + 8, :] = packed
        for c in range(nc):
            for p in planes:
                at = 2 * (p % 4)
                zsend[0, c, p // 4, at : at + 2, :] = grid[s, c, p + 2, 8:10, :]
                zsend[1, c, p // 4, at : at + 2, :] = grid[s, c, p + 2, 22:24, :]
            if 0 in planes:
                csend[0, c : c + 1, :] = grid[s, c, 2, 8:9, :]
                csend[1, c : c + 1, :] = grid[s, c, 2, 23:24, :]
            if 7 in planes:
                csend[2, c : c + 1, :] = grid[s, c, 9, 8:9, :]
                csend[3, c : c + 1, :] = grid[s, c, 9, 23:24, :]

    def shifted(s, p, nc):
        own = 0 <= p < 8
        slot, plane = (1, p) if own else ((0, 7) if p < 0 else (2, 0))
        for c in range(nc):
            k = c * 8 + plane
            for r in range(4):
                rows = slice(8 * r, 8 * r + 8)
                tile = grid[s, c, p + 2, rows, :]
                other = qrecv[s, slot, rows, :]
                if k:
                    other = pltpu.roll(other, 128 - 2 * k, 1)
                yp1[c, p + 2, rows, :] = pltpu.roll(jnp.where(seam[1], other, tile), 127, 1)
                ym1[c, p + 2, rows, :] = pltpu.roll(jnp.where(seam[-1], other, tile), 1, 1)
                if own and r in (1, 2):
                    yp2[c, p + 2, rows, :] = pltpu.roll(jnp.where(seam[2], other, tile), 126, 1)
                    ym2[c, p + 2, rows, :] = pltpu.roll(jnp.where(seam[-2], other, tile), 2, 1)

    def spread_near(s, nc):
        for c in range(nc):
            for p in range(8):
                at = 2 * (p % 4)
                grid[s, c, p + 2, 6:8, :] = zrecv[s, 0, c, p // 4, at : at + 2, :]
                grid[s, c, p + 2, 24:26, :] = zrecv[s, 1, c, p // 4, at : at + 2, :]
        for p in range(8):
            shifted(s, p, nc)

    def spread_far(s, nc):
        for c in range(nc):
            grid[s, c, 1, 7:8, :] = crecv[s, 0, c : c + 1, :]
            grid[s, c, 1, 24:25, :] = crecv[s, 1, c : c + 1, :]
            grid[s, c, 10, 7:8, :] = crecv[s, 2, c : c + 1, :]
            grid[s, c, 10, 24:25, :] = crecv[s, 3, c : c + 1, :]
        for p in (-1, 8):
            shifted(s, p, nc)

    def bonds(s, p, dirs, first, onto, x_inside=None):
        for t in range(2):
            mine = slice(8 * t, 8 * t + 8)
            base = slice(8 + 8 * t, 16 + 8 * t)
            centre = [grid[s, c, p + 2, base, :] for c in range(3)]
            moved = {}
            for c in range(3):
                for e in range(-2, 3):
                    moved[c, e] = centre[c] - float(e) if e else centre[c]
            if first:
                own_c, own_q = grid[s, 3, p + 2, base, :], grid[s, 4, p + 2, base, :]
            total = [acc[c, p, mine, :] for c in range(3)] if onto else [None] * 3
            for e in dirs:
                ex, ey, ez = e
                length = math.sqrt(ex * ex + ey * ey + ez * ez)
                rows = slice(8 + 8 * t + ez, 16 + 8 * t + ez)
                field = {1: yp1, -1: ym1, 2: yp2, -2: ym2}.get(ey)

                def near(c):
                    if field is None:
                        return grid[s, c, p + 2 + ex, rows, :]
                    return field[c, p + 2 + ex, rows, :]

                n = WHERE[e]
                if first:
                    a = (own_c + near(3)) * (0.5 / (length * length))
                    if x_inside is not None:
                        a = a * x_inside
                    if ey:
                        here = lane + (128 * gy + ey)
                        a = jnp.where((here >= 0) & (here < 256), a, 0.0)
                    if (t == 0 and ez < 0) or (t == 1 and ez > 0):
                        here = row + (16 * gz + 8 * t + ez)
                        a = jnp.where((here >= 0) & (here < 16 * nz), a, 0.0)
                    b = (-2.0 / (length * math.log(2.0))) / (own_q + near(4))
                    coef[n, 0, p, mine, :] = a
                    coef[n, 1, p, mine, :] = b
                else:
                    a = coef[n, 0, p, mine, :]
                    b = coef[n, 1, p, mine, :]
                sx = near(0) - moved[0, ex]
                sy = near(1) - moved[1, ey]
                sz = near(2) - moved[2, ez]
                square = jnp.maximum(sx * sx + sy * sy + sz * sz, TINY)
                inverse = lax.rsqrt(square)
                over = square * inverse - length
                pull = (a * over) * inverse * jnp.exp2(b * jnp.abs(over))
                for c, part in enumerate((sx, sy, sz)):
                    add = pull * part
                    total[c] = add if total[c] is None else total[c] + add
            for c in range(3):
                acc[c, p, mine, :] = total[c]

    inner = {
        0: [e for e in DIRS if e[0] >= 0],
        1: [e for e in DIRS if e[0] >= -1],
        6: [e for e in DIRS if e[0] <= 1],
        7: [e for e in DIRS if e[0] <= 0],
    }

    def near_bonds(s, first):
        for p in (0, 1, 6, 7):
            bonds(s, p, inner[p], first, False)

        def middle(p, carry):
            bonds(s, p, DIRS, first, False)
            return carry

        lax.fori_loop(2, 6, middle, 0)

    def far_bonds(s, first):
        for p in (0, 1, 6, 7):
            inside = None
            if first:
                inside = jnp.where(gx > 0, 1.0, 0.0) if p < 2 else jnp.where(gx < nx - 1, 1.0, 0.0)
            bonds(s, p, [e for e in DIRS if e not in inner[p]], first, True, inside)

    def advance(s, planes, weight):
        for p in planes:
            for c in range(3):
                new = free[p] * (speed[c, p] + weight * acc[c, p])
                speed[c, p] = new
                grid[1 - s, c, p + 2, 8:24, :] = grid[s, c, p + 2, 8:24, :] + DT * new

    near_by = lambda d: d[0] == 0
    far_off = lambda d: d[0] != 0

    loads[0].wait()
    for p in range(8):
        kind = cls[p]
        c_of = jnp.where(kind == 1, table_c[1], table_c[0])
        c_of = jnp.where(kind == 2, table_c[2], c_of)
        c_of = jnp.where(kind == 3, table_c[3], c_of)
        q_of = jnp.where(kind == 1, table_q[1], table_q[0])
        q_of = jnp.where(kind == 2, table_q[2], q_of)
        q_of = jnp.where(kind == 3, table_q[3], q_of)
        grid[0, 3, p + 2, 8:24, :] = c_of
        grid[0, 4, p + 2, 8:24, :] = q_of
    loads[1].wait()
    pack(0, range(8), 5, True)
    pl.semaphore_wait(barrier, NP)
    send_all(0, 5)
    loads[2].wait()
    loads[3].wait()
    for p in range(8):
        free[p] = 1.0 - clm[p].astype(jnp.float32)

    wait_from(0, 5, near_by)
    spread_near(0, 5)
    near_bonds(0, True)
    advance(0, range(2, 6), HALF)
    wait_sent(0, 5)
    pack(1, range(2, 6), 3, True)
    wait_from(0, 5, far_off)
    spread_far(0, 5)
    far_bonds(0, True)
    advance(0, (0, 1, 6, 7), HALF)
    pack(1, (0, 1, 6, 7), 3, False)
    send_all(1, 3)

    def step(k, carry):
        s = lax.rem(k, 2)
        weight = jnp.where(k == STEPS, HALF, DT)
        wait_from(s, 3, near_by)
        spread_near(s, 3)
        near_bonds(s, False)
        advance(s, range(2, 6), weight)
        wait_sent(s, 3)
        pack(1 - s, range(2, 6), 3, True)
        wait_from(s, 3, far_off)
        spread_far(s, 3)
        far_bonds(s, False)
        advance(s, (0, 1, 6, 7), weight)
        pack(1 - s, (0, 1, 6, 7), 3, False)

        @pl.when(k < STEPS)
        def _():
            send_all(1 - s, 3)

        return carry

    lax.fori_loop(1, STEPS + 1, step, 0)

    stores = [
        pltpu.make_async_copy(grid.at[STEPS % 2, 0:3, 2:10, 8:24], u_out, local_sem.at[1]),
        pltpu.make_async_copy(speed, v_out, local_sem.at[2]),
    ]
    for c in stores:
        c.start()
    for c in stores:
        c.wait()


def local(displacement, velocity, classes, clamped, stiffness, softening):
    block = displacement.shape
    f32 = jnp.float32
    anywhere = pl.BlockSpec(memory_space=pl.ANY)
    scalars = pl.BlockSpec(memory_space=pltpu.SMEM)
    return pl.pallas_call(
        kernel,
        out_shape=[jax.ShapeDtypeStruct(block, f32)] * 2,
        in_specs=[scalars, scalars] + [anywhere] * 4,
        out_specs=[anywhere] * 2,
        scratch_shapes=[
            pltpu.VMEM((2, 5, 12, 32, 128), f32),
            pltpu.VMEM((5, 12, 32, 128), f32),
            pltpu.VMEM((5, 12, 32, 128), f32),
            pltpu.VMEM((5, 12, 32, 128), f32),
            pltpu.VMEM((5, 12, 32, 128), f32),
            pltpu.VMEM((3, 8, 16, 128), f32),
            pltpu.VMEM((8, 16, 128), jnp.int32),
            pltpu.VMEM((8, 16, 128), jnp.int32),
            pltpu.VMEM((8, 16, 128), f32),
            pltpu.VMEM((3, 8, 16, 128), f32),
            pltpu.VMEM((len(DIRS), 2, 8, 16, 128), f32),
            pltpu.VMEM((2, 5, 2, 8, 128), f32),
            pltpu.VMEM((2, 2, 5, 2, 8, 128), f32),
            pltpu.VMEM((4, 8, 128), f32),
            pltpu.VMEM((2, 4, 8, 128), f32),
            pltpu.VMEM((16, 128), f32),
            pltpu.VMEM((2, 3, 32, 128), f32),
            pltpu.SemaphoreType.DMA((4,)),
            pltpu.SemaphoreType.DMA((NP,)),
            pltpu.SemaphoreType.DMA((2, NP)),
        ],
        compiler_params=pltpu.CompilerParams(collective_id=0, has_side_effects=True),
    )(stiffness, softening, displacement, velocity, classes, clamped)


def solution(mesh):
    return jax.shard_map(
        local,
        mesh=mesh,
        in_specs=(
            P(None, "gx", "gz", "gy"),
            P(None, "gx", "gz", "gy"),
            P("gx", "gz", "gy"),
            P("gx", "gz", "gy"),
            P(),
            P(),
        ),
        out_specs=(P(None, "gx", "gz", "gy"), P(None, "gx", "gz", "gy")),
        check_vma=False,
    )
```

```python
import math

import jax
import jax.numpy as jnp
from jax import lax
from jax.experimental import pallas as pl
from jax.experimental.pallas import tpu as pltpu
from jax.sharding import PartitionSpec as P

STEPS = 4
DT = 0.2
HALF = 0.1
MESH = pl.DeviceIdType.MESH

DIRS = [
    (ex, ey, ez)
    for ex in range(-2, 3)
    for ey in range(-2, 3)
    for ez in range(-2, 3)
    if 0 < ex * ex + ey * ey + ez * ez <= 4
]
WHERE = {e: n for n, e in enumerate(DIRS)}
PARTNERS = [
    (dx, dz, dy)
    for dx in (-1, 0, 1)
    for dz in (-1, 0, 1)
    for dy in (0, 1)
    if (dx, dz, dy) != (0, 0, 0)
]
SLOT = {d: n for n, d in enumerate(PARTNERS)}
NP = len(PARTNERS)
TINY = 1e-30


def opposite(d):
    return (-d[0], -d[1], d[2])


def kernel(
    table_c, table_q, u_in, v_in, class_in, clamp_in,
    u_out, v_out,
    grid, turned, speed, cls, clm, free, acc, coef,
    zsend, zrecv, csend, crecv, qsend, qrecv,
    local_sem, send_sem, recv_sem,
):
    gx, gy, gz = lax.axis_index("gx"), lax.axis_index("gy"), lax.axis_index("gz")
    nx, nz = lax.axis_size("gx"), lax.axis_size("gz")

    def device(d):
        return {
            "gx": lax.rem(gx + (d[0] + nx), nx),
            "gz": lax.rem(gz + (d[1] + nz), nz),
            "gy": 1 - gy if d[2] else gy,
        }

    has_left, has_right = gx > 0, gx < nx - 1

    def by_side(left, beside, right):
        pl.when(has_left)(left)
        beside()
        pl.when(has_right)(right)

    zero = jnp.zeros((8, 128), jnp.float32)
    for par in range(2):
        for r in range(4):
            rows = slice(8 * r, 8 * r + 8)
            for c in range(5):
                for plane in (0, 1, 10, 11):
                    grid[par, c, plane, rows, :] = zero
            qrecv[par, 0, rows, :] = zero
            qrecv[par, 2, rows, :] = zero
            crecv[par, r] = zero

    barrier = pltpu.get_barrier_semaphore()

    def greet(dx):
        def go():
            for d in PARTNERS:
                if d[0] == dx:
                    pl.semaphore_signal(barrier, inc=1, device_id=device(d), device_id_type=MESH)

        return go

    by_side(greet(-1), greet(0), greet(1))

    loads = [
        pltpu.make_async_copy(class_in, cls, local_sem.at[0]),
        pltpu.make_async_copy(u_in, grid.at[0, 0:3, 2:10, 8:24], local_sem.at[1]),
        pltpu.make_async_copy(v_in, speed, local_sem.at[2]),
        pltpu.make_async_copy(clamp_in, clm, local_sem.at[3]),
    ]
    for c in loads:
        c.start()

    lane = lax.broadcasted_iota(jnp.int32, (8, 128), 1)
    row = lax.broadcasted_iota(jnp.int32, (8, 128), 0)
    upper = gy == 1
    pair = lax.rem(lane - jnp.where(upper, 0, 126) + 128, 128) // 2
    from_other = {
        1: lane == jnp.where(upper, 0, 127),
        2: (lane >= jnp.where(upper, 0, 126)) & (lane < jnp.where(upper, 2, 128)),
    }
    swing = {1: jnp.where(upper, 1, 127), 2: jnp.where(upper, 2, 126)}

    def transfers(s, nc, which=lambda d: True):
        out = []
        for d in PARTNERS:
            if not which(d):
                continue
            dx, dz, dy = d
            m = SLOT[d]
            o = SLOT[opposite(d)]
            if d == (-1, 0, 0):
                src, dst = grid.at[s, 0:nc, 2:4, 8:24], grid.at[s, 0:nc, 10:12, 8:24]
            elif d == (1, 0, 0):
                src, dst = grid.at[s, 0:nc, 8:10, 8:24], grid.at[s, 0:nc, 0:2, 8:24]
            elif dy == 0 and dx == 0:
                side = 0 if dz < 0 else 1
                src, dst = zsend.at[side, 0:nc], zrecv.at[s, 1 - side, 0:nc]
            elif dy == 0:
                q = (0 if dx < 0 else 2) + (0 if dz < 0 else 1)
                src, dst = csend.at[q], crecv.at[s, 3 - q]
            else:
                if dz == 0:
                    src, dst = qsend.at[...], qrecv.at[s, 1 - dx, 8:24]
                elif dz > 0:
                    src, dst = qsend.at[8:16], qrecv.at[s, 1 - dx, 0:8]
                else:
                    src, dst = qsend.at[0:8], qrecv.at[s, 1 - dx, 24:32]
            out.append(
                pltpu.make_async_remote_copy(
                    src_ref=src,
                    dst_ref=dst,
                    send_sem=send_sem.at[m],
                    recv_sem=recv_sem.at[s, o],
                    device_id=device(d),
                    device_id_type=MESH,
                )
            )
        return out

    def each(s, nc, which, act):
        for t in transfers(s, nc, which):
            act(t)

    def start(s, nc, which):
        by_side(
            lambda: each(s, nc, lambda d: d[0] == -1 and which(d), lambda t: t.start()),
            lambda: each(s, nc, lambda d: d[0] == 0 and which(d), lambda t: t.start()),
            lambda: each(s, nc, lambda d: d[0] == 1 and which(d), lambda t: t.start()),
        )

    def wait_sent(s, nc):
        by_side(
            lambda: each(s, nc, lambda d: d[0] == -1, lambda t: t.wait_send()),
            lambda: each(s, nc, lambda d: d[0] == 0, lambda t: t.wait_send()),
            lambda: each(s, nc, lambda d: d[0] == 1, lambda t: t.wait_send()),
        )

    def wait_near(s, nc):
        each(s, nc, lambda d: d[0] == 0, lambda t: t.wait_recv())

    def wait_far(s, nc):
        pl.when(has_left)(lambda: each(s, nc, lambda d: d[0] == 1, lambda t: t.wait_recv()))
        pl.when(has_right)(lambda: each(s, nc, lambda d: d[0] == -1, lambda t: t.wait_recv()))

    def pack_corners(s, nc):
        for c in range(nc):
            csend[0, c : c + 1, :] = grid[s, c, 2, 8:9, :]
            csend[1, c : c + 1, :] = grid[s, c, 2, 23:24, :]
            csend[2, c : c + 1, :] = grid[s, c, 9, 8:9, :]
            csend[3, c : c + 1, :] = grid[s, c, 9, 23:24, :]

    def pack_columns(s, planes, nc, fresh):
        for t in range(2):
            packed = None if fresh else qsend[8 * t : 8 * t + 8, :]
            for c in range(nc):
                for p in planes:
                    k = c * 8 + p
                    tile = grid[s, c, p + 2, 8 + 8 * t : 16 + 8 * t, :]
                    moved = pltpu.roll(tile, 2 * k, 1) if k else tile
                    packed = moved if packed is None else jnp.where(pair == k, moved, packed)
            qsend[8 * t : 8 * t + 8, :] = packed

    def pack_rows(s, planes, nc):
        for c in range(nc):
            for p in planes:
                at = 2 * (p % 4)
                zsend[0, c, p // 4, at : at + 2, :] = grid[s, c, p + 2, 8:10, :]
                zsend[1, c, p // 4, at : at + 2, :] = grid[s, c, p + 2, 22:24, :]

    SHIFTS = ((0, 127), (1, 1), (2, 126), (3, 2))

    def turn_own(s, planes, nc, far):
        for c in range(nc):
            for p in planes:
                for r in (1, 2):
                    rows = slice(8 * r, 8 * r + 8)
                    tile = grid[s, c, p + 2, rows, :]
                    for n, by in SHIFTS[:2] if far else SHIFTS:
                        turned[n, c, p + 2, rows, :] = pltpu.roll(tile, by, 1)

    def turn_rows(s, planes, nc):
        for c in range(nc):
            for p in planes:
                ends = jnp.where(row < 4, grid[s, c, p + 2, 24:32, :], grid[s, c, p + 2, 0:8, :])
                for n, by in SHIFTS[:2]:
                    moved = pltpu.roll(ends, by, 1)
                    turned[n, c, p + 2, 0:8, :] = moved
                    turned[n, c, p + 2, 24:32, :] = moved

    def close_seam(s, planes, nc):
        for c in range(nc):
            for p in planes:
                slot, plane = (1, p) if 0 <= p < 8 else ((0, 7) if p < 0 else (2, 0))
                k = c * 8 + plane

                def other(tile, step):
                    return pltpu.roll(tile, lax.rem(swing[step] + (256 - 2 * k), 128), 1)

                ends = jnp.where(row < 4, qrecv[s, slot, 24:32, :], qrecv[s, slot, 0:8, :])
                ends = other(ends, 1)
                for r in range(4):
                    rows = slice(8 * r, 8 * r + 8)
                    inner_rows = r in (1, 2)
                    here = turned[gy, c, p + 2, rows, :]
                    there = other(qrecv[s, slot, rows, :], 1) if inner_rows else ends
                    turned[gy, c, p + 2, rows, :] = jnp.where(from_other[1], there, here)
                    if inner_rows and slot == 1:
                        here = turned[2 + gy, c, p + 2, rows, :]
                        there = other(qrecv[s, slot, rows, :], 2)
                        turned[2 + gy, c, p + 2, rows, :] = jnp.where(from_other[2], there, here)

    def spread_near(s, nc):
        for c in range(nc):
            for p in range(8):
                at = 2 * (p % 4)
                grid[s, c, p + 2, 6:8, :] = zrecv[s, 0, c, p // 4, at : at + 2, :]
                grid[s, c, p + 2, 24:26, :] = zrecv[s, 1, c, p // 4, at : at + 2, :]
        turn_rows(s, range(8), nc)
        close_seam(s, range(8), nc)

    def spread_far(s, nc):
        for c in range(nc):
            grid[s, c, 1, 7:8, :] = crecv[s, 0, c : c + 1, :]
            grid[s, c, 1, 24:25, :] = crecv[s, 1, c : c + 1, :]
            grid[s, c, 10, 7:8, :] = crecv[s, 2, c : c + 1, :]
            grid[s, c, 10, 24:25, :] = crecv[s, 3, c : c + 1, :]
        turn_own(s, (-1, 8), nc, True)
        turn_rows(s, (-1, 8), nc)
        close_seam(s, (-1, 8), nc)

    def needs_near(e, t):
        return bool(e[1]) or (t == 0 and e[2] < 0) or (t == 1 and e[2] > 0)

    def bonds(s, p, dirs, first, onto, x_inside=None, part=None):
        for t in range(2):
            chosen = [e for e in dirs if part is None or needs_near(e, t) == part]
            mine = slice(8 * t, 8 * t + 8)
            base = slice(8 + 8 * t, 16 + 8 * t)
            centre = [grid[s, c, p + 2, base, :] for c in range(3)]
            moved = {}
            for c in range(3):
                for e in range(-2, 3):
                    moved[c, e] = centre[c] - float(e) if e else centre[c]
            if first:
                own_c, own_q = grid[s, 3, p + 2, base, :], grid[s, 4, p + 2, base, :]
            total = [acc[c, p, mine, :] for c in range(3)] if onto else [None] * 3
            for e in chosen:
                ex, ey, ez = e
                length = math.sqrt(ex * ex + ey * ey + ez * ez)
                rows = slice(8 + 8 * t + ez, 16 + 8 * t + ez)
                field = {1: 0, -1: 1, 2: 2, -2: 3}.get(ey)

                def near(c):
                    if field is None:
                        return grid[s, c, p + 2 + ex, rows, :]
                    return turned[field, c, p + 2 + ex, rows, :]

                n = WHERE[e]
                if first:
                    a = (own_c + near(3)) * (0.5 / (length * length))
                    if x_inside is not None:
                        a = a * x_inside
                    if ey:
                        here = lane + (128 * gy + ey)
                        a = jnp.where((here >= 0) & (here < 256), a, 0.0)
                    if (t == 0 and ez < 0) or (t == 1 and ez > 0):
                        here = row + (16 * gz + 8 * t + ez)
                        a = jnp.where((here >= 0) & (here < 16 * nz), a, 0.0)
                    b = (-2.0 / (length * math.log(2.0))) / (own_q + near(4))
                    coef[n, 0, p, mine, :] = a
                    coef[n, 1, p, mine, :] = b
                else:
                    a = coef[n, 0, p, mine, :]
                    b = coef[n, 1, p, mine, :]
                sx = near(0) - moved[0, ex]
                sy = near(1) - moved[1, ey]
                sz = near(2) - moved[2, ez]
                square = jnp.maximum(sx * sx + sy * sy + sz * sz, TINY)
                inverse = lax.rsqrt(square)
                over = square * inverse - length
                pull = (a * over) * inverse * jnp.exp2(b * jnp.abs(over))
                for c, way in enumerate((sx, sy, sz)):
                    add = pull * way
                    total[c] = add if total[c] is None else total[c] + add
            for c in range(3):
                acc[c, p, mine, :] = total[c]

    inner = {
        0: [e for e in DIRS if e[0] >= 0],
        1: [e for e in DIRS if e[0] >= -1],
        6: [e for e in DIRS if e[0] <= 1],
        7: [e for e in DIRS if e[0] <= 0],
    }

    def near_bonds(s, first, part):
        for p in (0, 1, 6, 7):
            bonds(s, p, inner[p], first, part, part=part)

        def middle(p, carry):
            bonds(s, p, DIRS, first, part, part=part)
            return carry

        lax.fori_loop(2, 6, middle, 0)

    def far_bonds(s, first):
        for p in (0, 1, 6, 7):
            inside = None
            if first:
                inside = jnp.where(gx > 0, 1.0, 0.0) if p < 2 else jnp.where(gx < nx - 1, 1.0, 0.0)
            bonds(s, p, [e for e in DIRS if e not in inner[p]], first, True, inside)

    def advance(s, planes, weight):
        for p in planes:
            for c in range(3):
                new = free[p] * (speed[c, p] + weight * acc[c, p])
                speed[c, p] = new
                grid[1 - s, c, p + 2, 8:24, :] = grid[s, c, p + 2, 8:24, :] + DT * new

    def send(s, nc):
        pack_corners(s, nc)
        start(s, nc, lambda d: d[2] == 0 and d[0])
        pack_columns(s, (0, 1, 6, 7), nc, False)
        start(s, nc, lambda d: d[2] == 1)
        pack_rows(s, (0, 1, 6, 7), nc)
        start(s, nc, lambda d: d[2] == 0 and not d[0])

    def run(s, nc, first, weight, go_on):
        turn_own(s, range(8), nc, False)
        near_bonds(s, first, False)
        wait_near(s, nc)
        spread_near(s, nc)
        near_bonds(s, first, True)
        advance(s, range(2, 6), weight)
        wait_sent(s, nc)
        go_on(lambda: (pack_columns(1 - s, range(2, 6), 3, True), pack_rows(1 - s, range(2, 6), 3)))
        wait_far(s, nc)
        spread_far(s, nc)
        far_bonds(s, first)
        advance(s, (0, 1, 6, 7), weight)
        go_on(lambda: send(1 - s, 3))

    loads[0].wait()
    for p in range(8):
        kind = cls[p]
        c_of = jnp.where(kind == 1, table_c[1], table_c[0])
        c_of = jnp.where(kind == 2, table_c[2], c_of)
        c_of = jnp.where(kind == 3, table_c[3], c_of)
        q_of = jnp.where(kind == 1, table_q[1], table_q[0])
        q_of = jnp.where(kind == 2, table_q[2], q_of)
        q_of = jnp.where(kind == 3, table_q[3], q_of)
        grid[0, 3, p + 2, 8:24, :] = c_of
        grid[0, 4, p + 2, 8:24, :] = q_of
    loads[1].wait()
    pack_columns(0, range(2, 6), 5, True)
    pack_rows(0, range(2, 6), 5)
    pl.semaphore_wait(barrier, 5 + jnp.where(has_left, 6, 0) + jnp.where(has_right, 6, 0))
    send(0, 5)
    loads[2].wait()
    loads[3].wait()
    for p in range(8):
        free[p] = 1.0 - clm[p].astype(jnp.float32)

    run(0, 5, True, HALF, lambda f: f())

    def step(k, carry):
        weight = jnp.where(k == STEPS, HALF, DT)

        def go_on(f):
            @pl.when(k < STEPS)
            def _():
                f()

        run(lax.rem(k, 2), 3, False, weight, go_on)
        return carry

    lax.fori_loop(1, STEPS + 1, step, 0)

    stores = [
        pltpu.make_async_copy(grid.at[STEPS % 2, 0:3, 2:10, 8:24], u_out, local_sem.at[1]),
        pltpu.make_async_copy(speed, v_out, local_sem.at[2]),
    ]
    for c in stores:
        c.start()
    for c in stores:
        c.wait()


def local(displacement, velocity, classes, clamped, stiffness, softening):
    block = displacement.shape
    f32 = jnp.float32
    anywhere = pl.BlockSpec(memory_space=pl.ANY)
    scalars = pl.BlockSpec(memory_space=pltpu.SMEM)
    return pl.pallas_call(
        kernel,
        out_shape=[jax.ShapeDtypeStruct(block, f32)] * 2,
        in_specs=[scalars, scalars] + [anywhere] * 4,
        out_specs=[anywhere] * 2,
        scratch_shapes=[
            pltpu.VMEM((2, 5, 12, 32, 128), f32),
            pltpu.VMEM((4, 5, 12, 32, 128), f32),
            pltpu.VMEM((3, 8, 16, 128), f32),
            pltpu.VMEM((8, 16, 128), jnp.int32),
            pltpu.VMEM((8, 16, 128), jnp.int32),
            pltpu.VMEM((8, 16, 128), f32),
            pltpu.VMEM((3, 8, 16, 128), f32),
            pltpu.VMEM((len(DIRS), 2, 8, 16, 128), f32),
            pltpu.VMEM((2, 5, 2, 8, 128), f32),
            pltpu.VMEM((2, 2, 5, 2, 8, 128), f32),
            pltpu.VMEM((4, 8, 128), f32),
            pltpu.VMEM((2, 4, 8, 128), f32),
            pltpu.VMEM((16, 128), f32),
            pltpu.VMEM((2, 3, 32, 128), f32),
            pltpu.SemaphoreType.DMA((4,)),
            pltpu.SemaphoreType.DMA((NP,)),
            pltpu.SemaphoreType.DMA((2, NP)),
        ],
        compiler_params=pltpu.CompilerParams(collective_id=0, has_side_effects=True),
    )(stiffness, softening, displacement, velocity, classes, clamped)


def solution(mesh):
    return jax.shard_map(
        local,
        mesh=mesh,
        in_specs=(
            P(None, "gx", "gz", "gy"),
            P(None, "gx", "gz", "gy"),
            P("gx", "gz", "gy"),
            P("gx", "gz", "gy"),
            P(),
            P(),
        ),
        out_specs=(P(None, "gx", "gz", "gy"), P(None, "gx", "gz", "gy")),
        check_vma=False,
    )
```

```python
import math

import jax
import jax.numpy as jnp
from jax import lax
from jax.experimental import pallas as pl
from jax.experimental.pallas import tpu as pltpu
from jax.sharding import PartitionSpec as P

STEPS = 4
DT = 0.2
HALF = 0.1
MESH = pl.DeviceIdType.MESH

DIRS = [
    (ex, ey, ez)
    for ex in range(-2, 3)
    for ey in range(-2, 3)
    for ez in range(-2, 3)
    if 0 < ex * ex + ey * ey + ez * ez <= 4
]
WHERE = {e: n for n, e in enumerate(DIRS)}
PARTNERS = [
    (dx, dz, dy)
    for dx in (-1, 0, 1)
    for dz in (-1, 0, 1)
    for dy in (0, 1)
    if (dx, dz, dy) != (0, 0, 0)
]
SLOT = {d: n for n, d in enumerate(PARTNERS)}
NP = len(PARTNERS)
TINY = 1e-30


def opposite(d):
    return (-d[0], -d[1], d[2])


def kernel(
    table_c_in, table_q_in, u_in, v_in, class_in, clamp_in,
    u_out, v_out,
    table_c, table_q, grid, turned, speed, cls, clm, free, acc, coef,
    zsend, zrecv, csend, crecv, qsend, qrecv,
    local_sem, send_sem, recv_sem,
):
    gx, gy, gz = lax.axis_index("gx"), lax.axis_index("gy"), lax.axis_index("gz")
    nx, nz = lax.axis_size("gx"), lax.axis_size("gz")

    def device(d):
        return {
            "gx": lax.rem(gx + (d[0] + nx), nx),
            "gz": lax.rem(gz + (d[1] + nz), nz),
            "gy": 1 - gy if d[2] else gy,
        }

    has_left, has_right = gx > 0, gx < nx - 1

    def by_side(left, beside, right):
        pl.when(has_left)(left)
        beside()
        pl.when(has_right)(right)

    zero = jnp.zeros((8, 128), jnp.float32)
    for par in range(2):
        for r in range(4):
            rows = slice(8 * r, 8 * r + 8)
            for c in range(5):
                for plane in (0, 1, 10, 11):
                    grid[par, c, plane, rows, :] = zero
            qrecv[par, 0, rows, :] = zero
            qrecv[par, 2, rows, :] = zero
            crecv[par, r] = zero

    barrier = pltpu.get_barrier_semaphore()

    def greet(dx):
        def go():
            for d in PARTNERS:
                if d[0] == dx:
                    pl.semaphore_signal(barrier, inc=1, device_id=device(d), device_id_type=MESH)

        return go

    by_side(greet(-1), greet(0), greet(1))

    loads = [
        pltpu.make_async_copy(class_in, cls, local_sem.at[0]),
        pltpu.make_async_copy(u_in, grid.at[0, 0:3, 2:10, 8:24], local_sem.at[1]),
        pltpu.make_async_copy(v_in, speed, local_sem.at[2]),
        pltpu.make_async_copy(clamp_in, clm, local_sem.at[3]),
        pltpu.make_async_copy(table_c_in, table_c, local_sem.at[4]),
        pltpu.make_async_copy(table_q_in, table_q, local_sem.at[5]),
    ]
    for c in loads:
        c.start()

    lane = lax.broadcasted_iota(jnp.int32, (8, 128), 1)
    row = lax.broadcasted_iota(jnp.int32, (8, 128), 0)
    upper = gy == 1
    pair = lax.rem(lane - jnp.where(upper, 0, 126) + 128, 128) // 2
    from_other = {
        1: lane == jnp.where(upper, 0, 127),
        2: (lane >= jnp.where(upper, 0, 126)) & (lane < jnp.where(upper, 2, 128)),
    }
    swing = {1: jnp.where(upper, 1, 127), 2: jnp.where(upper, 2, 126)}

    def transfers(s, nc, which=lambda d: True):
        out = []
        for d in PARTNERS:
            if not which(d):
                continue
            dx, dz, dy = d
            m = SLOT[d]
            o = SLOT[opposite(d)]
            if d == (-1, 0, 0):
                src, dst = grid.at[s, 0:nc, 2:4, 8:24], grid.at[s, 0:nc, 10:12, 8:24]
            elif d == (1, 0, 0):
                src, dst = grid.at[s, 0:nc, 8:10, 8:24], grid.at[s, 0:nc, 0:2, 8:24]
            elif dy == 0 and dx == 0:
                side = 0 if dz < 0 else 1
                src, dst = zsend.at[side, 0:nc], zrecv.at[s, 1 - side, 0:nc]
            elif dy == 0:
                q = (0 if dx < 0 else 2) + (0 if dz < 0 else 1)
                src, dst = csend.at[q], crecv.at[s, 3 - q]
            else:
                if dz == 0:
                    src, dst = qsend.at[...], qrecv.at[s, 1 - dx, 8:24]
                elif dz > 0:
                    src, dst = qsend.at[8:16], qrecv.at[s, 1 - dx, 0:8]
                else:
                    src, dst = qsend.at[0:8], qrecv.at[s, 1 - dx, 24:32]
            out.append(
                pltpu.make_async_remote_copy(
                    src_ref=src,
                    dst_ref=dst,
                    send_sem=send_sem.at[m],
                    recv_sem=recv_sem.at[s, o],
                    device_id=device(d),
                    device_id_type=MESH,
                )
            )
        return out

    def each(s, nc, which, act):
        for t in transfers(s, nc, which):
            act(t)

    def start(s, nc, which):
        def go(dx):
            return lambda: each(s, nc, lambda d: d[0] == dx and which(d), lambda t: t.start())

        if any(d[0] and which(d) for d in PARTNERS):
            by_side(go(-1), go(0), go(1))
        else:
            go(0)()

    def wait_sent(s, nc):
        by_side(
            lambda: each(s, nc, lambda d: d[0] == -1, lambda t: t.wait_send()),
            lambda: each(s, nc, lambda d: d[0] == 0, lambda t: t.wait_send()),
            lambda: each(s, nc, lambda d: d[0] == 1, lambda t: t.wait_send()),
        )

    def wait_beside(s, nc):
        each(s, nc, lambda d: d == (0, 0, 1), lambda t: t.wait_recv())

    def wait_rows(s, nc):
        each(s, nc, lambda d: d[0] == 0 and d[1], lambda t: t.wait_recv())

    def wait_far(s, nc):
        pl.when(has_left)(lambda: each(s, nc, lambda d: d[0] == 1, lambda t: t.wait_recv()))
        pl.when(has_right)(lambda: each(s, nc, lambda d: d[0] == -1, lambda t: t.wait_recv()))

    def pack_corners(s, nc):
        for c in range(nc):
            csend[0, c : c + 1, :] = grid[s, c, 2, 8:9, :]
            csend[1, c : c + 1, :] = grid[s, c, 2, 23:24, :]
            csend[2, c : c + 1, :] = grid[s, c, 9, 8:9, :]
            csend[3, c : c + 1, :] = grid[s, c, 9, 23:24, :]

    def pack_columns(s, planes, nc, fresh):
        for t in range(2):
            packed = None if fresh else qsend[8 * t : 8 * t + 8, :]
            for c in range(nc):
                for p in planes:
                    k = c * 8 + p
                    tile = grid[s, c, p + 2, 8 + 8 * t : 16 + 8 * t, :]
                    moved = pltpu.roll(tile, 2 * k, 1) if k else tile
                    packed = moved if packed is None else jnp.where(pair == k, moved, packed)
            qsend[8 * t : 8 * t + 8, :] = packed

    def pack_rows(s, planes, nc):
        for c in range(nc):
            for p in planes:
                at = 2 * (p % 4)
                zsend[0, c, p // 4, at : at + 2, :] = grid[s, c, p + 2, 8:10, :]
                zsend[1, c, p // 4, at : at + 2, :] = grid[s, c, p + 2, 22:24, :]

    SHIFTS = ((0, 127), (1, 1), (2, 126), (3, 2))

    def turn_own(s, planes, nc, far):
        for c in range(nc):
            for p in planes:
                for r in (1, 2):
                    rows = slice(8 * r, 8 * r + 8)
                    tile = grid[s, c, p + 2, rows, :]
                    for n, by in SHIFTS[:2] if far else SHIFTS:
                        turned[n, c, p + 2, rows, :] = pltpu.roll(tile, by, 1)

    def turn_rows(s, planes, nc):
        for c in range(nc):
            for p in planes:
                ends = jnp.where(row < 4, grid[s, c, p + 2, 24:32, :], grid[s, c, p + 2, 0:8, :])
                for n, by in SHIFTS[:2]:
                    moved = pltpu.roll(ends, by, 1)
                    turned[n, c, p + 2, 0:8, :] = moved
                    turned[n, c, p + 2, 24:32, :] = moved

    def close_seam(s, planes, nc, tiles=(0, 1, 2, 3)):
        for c in range(nc):
            for p in planes:
                slot, plane = (1, p) if 0 <= p < 8 else ((0, 7) if p < 0 else (2, 0))
                k = c * 8 + plane

                def other(tile, step):
                    return pltpu.roll(tile, lax.rem(swing[step] + (256 - 2 * k), 128), 1)

                if 0 in tiles:
                    ends = jnp.where(row < 4, qrecv[s, slot, 24:32, :], qrecv[s, slot, 0:8, :])
                    ends = other(ends, 1)
                for r in tiles:
                    rows = slice(8 * r, 8 * r + 8)
                    inner_rows = r in (1, 2)
                    here = turned[gy, c, p + 2, rows, :]
                    there = other(qrecv[s, slot, rows, :], 1) if inner_rows else ends
                    turned[gy, c, p + 2, rows, :] = jnp.where(from_other[1], there, here)
                    if inner_rows and slot == 1:
                        here = turned[2 + gy, c, p + 2, rows, :]
                        there = other(qrecv[s, slot, rows, :], 2)
                        turned[2 + gy, c, p + 2, rows, :] = jnp.where(from_other[2], there, here)

    def spread_near(s, nc):
        for c in range(nc):
            for p in range(8):
                at = 2 * (p % 4)
                grid[s, c, p + 2, 6:8, :] = zrecv[s, 0, c, p // 4, at : at + 2, :]
                grid[s, c, p + 2, 24:26, :] = zrecv[s, 1, c, p // 4, at : at + 2, :]
        turn_rows(s, range(8), nc)
        close_seam(s, range(8), nc, (0, 3))

    def spread_far(s, nc):
        for c in range(nc):
            grid[s, c, 1, 7:8, :] = crecv[s, 0, c : c + 1, :]
            grid[s, c, 1, 24:25, :] = crecv[s, 1, c : c + 1, :]
            grid[s, c, 10, 7:8, :] = crecv[s, 2, c : c + 1, :]
            grid[s, c, 10, 24:25, :] = crecv[s, 3, c : c + 1, :]
        turn_own(s, (-1, 8), nc, True)
        turn_rows(s, (-1, 8), nc)
        close_seam(s, (-1, 8), nc)

    def needs_near(e, t):
        return 2 if (t == 0 and e[2] < 0) or (t == 1 and e[2] > 0) else 1 if e[1] else 0

    def bonds(s, p, dirs, first, onto, x_inside=None, part=None):
        for t in range(2):
            chosen = [e for e in dirs if part is None or needs_near(e, t) == part]
            mine = slice(8 * t, 8 * t + 8)
            base = slice(8 + 8 * t, 16 + 8 * t)
            centre = [grid[s, c, p + 2, base, :] for c in range(3)]
            moved = {}
            for c in range(3):
                for e in range(-2, 3):
                    moved[c, e] = centre[c] - float(e) if e else centre[c]
            if first:
                own_c, own_q = grid[s, 3, p + 2, base, :], grid[s, 4, p + 2, base, :]
            total = [acc[c, p, mine, :] for c in range(3)] if onto else [None] * 3
            for e in chosen:
                ex, ey, ez = e
                length = math.sqrt(ex * ex + ey * ey + ez * ez)
                rows = slice(8 + 8 * t + ez, 16 + 8 * t + ez)
                field = {1: 0, -1: 1, 2: 2, -2: 3}.get(ey)

                def near(c):
                    if field is None:
                        return grid[s, c, p + 2 + ex, rows, :]
                    return turned[field, c, p + 2 + ex, rows, :]

                n = WHERE[e]
                if first:
                    a = (own_c + near(3)) * (0.5 / (length * length))
                    if x_inside is not None:
                        a = a * x_inside
                    if ey:
                        here = lane + (128 * gy + ey)
                        a = jnp.where((here >= 0) & (here < 256), a, 0.0)
                    if (t == 0 and ez < 0) or (t == 1 and ez > 0):
                        here = row + (16 * gz + 8 * t + ez)
                        a = jnp.where((here >= 0) & (here < 16 * nz), a, 0.0)
                    b = (-2.0 / (length * math.log(2.0))) / (own_q + near(4))
                    coef[n, 0, p, mine, :] = a
                    coef[n, 1, p, mine, :] = b
                else:
                    a = coef[n, 0, p, mine, :]
                    b = coef[n, 1, p, mine, :]
                sx = near(0) - moved[0, ex]
                sy = near(1) - moved[1, ey]
                sz = near(2) - moved[2, ez]
                square = jnp.maximum(sx * sx + sy * sy + sz * sz, TINY)
                inverse = lax.rsqrt(square)
                over = square * inverse - length
                pull = (a * over) * inverse * jnp.exp2(b * jnp.abs(over))
                for c, way in enumerate((sx, sy, sz)):
                    add = pull * way
                    total[c] = add if total[c] is None else total[c] + add
            for c in range(3):
                acc[c, p, mine, :] = total[c]

    inner = {
        0: [e for e in DIRS if e[0] >= 0],
        1: [e for e in DIRS if e[0] >= -1],
        6: [e for e in DIRS if e[0] <= 1],
        7: [e for e in DIRS if e[0] <= 0],
    }

    def near_bonds(s, first, part):
        for p in (0, 1, 6, 7):
            bonds(s, p, inner[p], first, part > 0, part=part)

        def middle(p, carry):
            bonds(s, p, DIRS, first, part > 0, part=part)
            return carry

        lax.fori_loop(2, 6, middle, 0)

    def far_bonds(s, first):
        for p in (0, 1, 6, 7):
            inside = None
            if first:
                inside = jnp.where(gx > 0, 1.0, 0.0) if p < 2 else jnp.where(gx < nx - 1, 1.0, 0.0)
            bonds(s, p, [e for e in DIRS if e not in inner[p]], first, True, inside)

    def advance(s, planes, weight):
        for p in planes:
            for c in range(3):
                new = free[p] * (speed[c, p] + weight * acc[c, p])
                speed[c, p] = new
                grid[1 - s, c, p + 2, 8:24, :] = grid[s, c, p + 2, 8:24, :] + DT * new

    def send(s, nc):
        pack_corners(s, nc)
        start(s, nc, lambda d: d[0] and d[1] and not d[2])
        pack_columns(s, (0, 1, 6, 7), nc, False)
        start(s, nc, lambda d: d[0] and d[2])
        start(s, nc, lambda d: not d[0] and d[2])
        start(s, nc, lambda d: d[0] and not d[1] and not d[2])
        pack_rows(s, (0, 1, 6, 7), nc)
        start(s, nc, lambda d: not d[0] and not d[2])

    def run(s, nc, first, weight, go_on):
        turn_own(s, range(8), nc, False)
        near_bonds(s, first, 0)
        wait_beside(s, nc)
        close_seam(s, range(8), nc, (1, 2))
        near_bonds(s, first, 1)
        wait_rows(s, nc)
        spread_near(s, nc)
        near_bonds(s, first, 2)
        advance(s, range(2, 6), weight)
        wait_sent(s, nc)
        go_on(lambda: (pack_columns(1 - s, range(2, 6), 3, True), pack_rows(1 - s, range(2, 6), 3)))
        wait_far(s, nc)
        spread_far(s, nc)
        far_bonds(s, first)
        advance(s, (0, 1, 6, 7), weight)
        go_on(lambda: send(1 - s, 3))

    loads[4].wait()
    loads[5].wait()
    loads[0].wait()
    for p in range(8):
        kind = cls[p]
        c_of = jnp.where(kind == 1, table_c[1], table_c[0])
        c_of = jnp.where(kind == 2, table_c[2], c_of)
        c_of = jnp.where(kind == 3, table_c[3], c_of)
        q_of = jnp.where(kind == 1, table_q[1], table_q[0])
        q_of = jnp.where(kind == 2, table_q[2], q_of)
        q_of = jnp.where(kind == 3, table_q[3], q_of)
        grid[0, 3, p + 2, 8:24, :] = c_of
        grid[0, 4, p + 2, 8:24, :] = q_of
    loads[1].wait()
    pack_columns(0, range(2, 6), 5, True)
    pack_rows(0, range(2, 6), 5)
    pl.semaphore_wait(barrier, 5 + jnp.where(has_left, 6, 0) + jnp.where(has_right, 6, 0))
    send(0, 5)
    loads[2].wait()
    loads[3].wait()
    for p in range(8):
        free[p] = 1.0 - clm[p].astype(jnp.float32)

    run(0, 5, True, HALF, lambda f: f())

    stores = [
        pltpu.make_async_copy(grid.at[STEPS % 2, 0:3, 2:10, 8:24], u_out, local_sem.at[1]),
        pltpu.make_async_copy(speed, v_out, local_sem.at[2]),
    ]

    def step(k, carry):
        weight = jnp.where(k == STEPS, HALF, DT)

        def go_on(f):
            @pl.when(k < STEPS)
            def _():
                f()

        @pl.when(k == STEPS)
        def _():
            stores[0].start()

        run(lax.rem(k, 2), 3, False, weight, go_on)
        return carry

    lax.fori_loop(1, STEPS + 1, step, 0)

    stores[1].start()
    for c in stores:
        c.wait()


def local(displacement, velocity, classes, clamped, stiffness, softening):
    block = displacement.shape
    f32 = jnp.float32
    anywhere = pl.BlockSpec(memory_space=pl.ANY)
    outside = pl.BlockSpec(memory_space=pltpu.HBM)
    return pl.pallas_call(
        kernel,
        out_shape=[jax.ShapeDtypeStruct(block, f32)] * 2,
        in_specs=[outside] * 6,
        out_specs=[anywhere] * 2,
        scratch_shapes=[
            pltpu.SMEM((4,), f32),
            pltpu.SMEM((4,), f32),
            pltpu.VMEM((2, 5, 12, 32, 128), f32),
            pltpu.VMEM((4, 5, 12, 32, 128), f32),
            pltpu.VMEM((3, 8, 16, 128), f32),
            pltpu.VMEM((8, 16, 128), jnp.int32),
            pltpu.VMEM((8, 16, 128), jnp.int32),
            pltpu.VMEM((8, 16, 128), f32),
            pltpu.VMEM((3, 8, 16, 128), f32),
            pltpu.VMEM((len(DIRS), 2, 8, 16, 128), f32),
            pltpu.VMEM((2, 5, 2, 8, 128), f32),
            pltpu.VMEM((2, 2, 5, 2, 8, 128), f32),
            pltpu.VMEM((4, 8, 128), f32),
            pltpu.VMEM((2, 4, 8, 128), f32),
            pltpu.VMEM((16, 128), f32),
            pltpu.VMEM((2, 3, 32, 128), f32),
            pltpu.SemaphoreType.DMA((6,)),
            pltpu.SemaphoreType.DMA((NP,)),
            pltpu.SemaphoreType.DMA((2, NP)),
        ],
        compiler_params=pltpu.CompilerParams(collective_id=0, has_side_effects=True, vmem_limit_bytes=15 << 20),
    )(*(pltpu.with_memory_space_constraint(x, pltpu.HBM) for x in (stiffness, softening, displacement, velocity, classes, clamped)))


def solution(mesh):
    return jax.shard_map(
        local,
        mesh=mesh,
        in_specs=(
            P(None, "gx", "gz", "gy"),
            P(None, "gx", "gz", "gy"),
            P("gx", "gz", "gy"),
            P("gx", "gz", "gy"),
            P(),
            P(),
        ),
        out_specs=(P(None, "gx", "gz", "gy"), P(None, "gx", "gz", "gy")),
        check_vma=False,
    )
```

```python
import math

import jax
import jax.numpy as jnp
from jax import lax
from jax.experimental import pallas as pl
from jax.experimental.pallas import tpu as pltpu
from jax.sharding import PartitionSpec as P

STEPS = 4
DT = 0.2
HALF = 0.1
MESH = pl.DeviceIdType.MESH

DIRS = [
    (ex, ey, ez)
    for ex in range(-2, 3)
    for ey in range(-2, 3)
    for ez in range(-2, 3)
    if 0 < ex * ex + ey * ey + ez * ez <= 4
]
WHERE = {e: n for n, e in enumerate(DIRS)}
PARTNERS = [
    (dx, dz, dy)
    for dx in (-1, 0, 1)
    for dz in (-1, 0, 1)
    for dy in (0, 1)
    if (dx, dz, dy) != (0, 0, 0)
]
SLOT = {d: n for n, d in enumerate(PARTNERS)}
NP = len(PARTNERS)
TINY = 1e-30


def opposite(d):
    return (-d[0], -d[1], d[2])


def kernel(
    table_c_in, table_q_in, u_in, v_in, class_in, clamp_in,
    u_out, v_out,
    table_c, table_q, grid, turned, speed, cls, clm, free, acc, coef,
    zsend, zrecv, csend, crecv, qsend, qrecv,
    local_sem, send_sem, recv_sem,
):
    gx, gy, gz = lax.axis_index("gx"), lax.axis_index("gy"), lax.axis_index("gz")
    nx, nz = lax.axis_size("gx"), lax.axis_size("gz")

    def device(d):
        return {
            "gx": lax.rem(gx + (d[0] + nx), nx),
            "gz": lax.rem(gz + (d[1] + nz), nz),
            "gy": 1 - gy if d[2] else gy,
        }

    has_left, has_right = gx > 0, gx < nx - 1

    def by_side(left, beside, right):
        pl.when(has_left)(left)
        beside()
        pl.when(has_right)(right)

    barrier = pltpu.get_barrier_semaphore()

    def greet(dx):
        def go():
            for d in PARTNERS:
                if d[0] == dx:
                    pl.semaphore_signal(barrier, inc=1, device_id=device(d), device_id_type=MESH)

        return go

    by_side(greet(-1), greet(0), greet(1))

    zero = jnp.zeros((8, 128), jnp.float32)

    def clear(planes, slot, corners):
        def go():
            for par in range(2):
                for r in range(4):
                    rows = slice(8 * r, 8 * r + 8)
                    for c in range(5):
                        for plane in planes:
                            grid[par, c, plane, rows, :] = zero
                    qrecv[par, slot, rows, :] = zero
                for q in corners:
                    crecv[par, q] = zero

        return go

    pl.when(jnp.logical_not(has_left))(clear((0, 1), 0, (0, 1)))
    pl.when(jnp.logical_not(has_right))(clear((10, 11), 2, (2, 3)))

    loads = [
        pltpu.make_async_copy(class_in, cls, local_sem.at[0]),
        pltpu.make_async_copy(u_in, grid.at[0, 0:3, 2:10, 8:24], local_sem.at[1]),
        pltpu.make_async_copy(v_in, speed, local_sem.at[2]),
        pltpu.make_async_copy(clamp_in, clm, local_sem.at[3]),
        pltpu.make_async_copy(table_c_in, table_c, local_sem.at[4]),
        pltpu.make_async_copy(table_q_in, table_q, local_sem.at[5]),
    ]
    for c in loads:
        c.start()

    lane = lax.broadcasted_iota(jnp.int32, (8, 128), 1)
    row = lax.broadcasted_iota(jnp.int32, (8, 128), 0)
    upper = gy == 1
    pair = lax.rem(lane - jnp.where(upper, 0, 126) + 128, 128) // 2
    from_other = {
        1: lane == jnp.where(upper, 0, 127),
        2: (lane >= jnp.where(upper, 0, 126)) & (lane < jnp.where(upper, 2, 128)),
    }
    swing = {1: jnp.where(upper, 1, 127), 2: jnp.where(upper, 2, 126)}

    def transfers(s, nc, which=lambda d: True):
        out = []
        for d in PARTNERS:
            if not which(d):
                continue
            dx, dz, dy = d
            m = SLOT[d]
            o = SLOT[opposite(d)]
            if d == (-1, 0, 0):
                src, dst = grid.at[s, 0:nc, 2:4, 8:24], grid.at[s, 0:nc, 10:12, 8:24]
            elif d == (1, 0, 0):
                src, dst = grid.at[s, 0:nc, 8:10, 8:24], grid.at[s, 0:nc, 0:2, 8:24]
            elif dy == 0 and dx == 0:
                side = 0 if dz < 0 else 1
                src, dst = zsend.at[side, 0:nc], zrecv.at[s, 1 - side, 0:nc]
            elif dy == 0:
                q = (0 if dx < 0 else 2) + (0 if dz < 0 else 1)
                src, dst = csend.at[q], crecv.at[s, 3 - q]
            else:
                if dz == 0:
                    src, dst = qsend.at[...], qrecv.at[s, 1 - dx, 8:24]
                elif dz > 0:
                    src, dst = qsend.at[8:16], qrecv.at[s, 1 - dx, 0:8]
                else:
                    src, dst = qsend.at[0:8], qrecv.at[s, 1 - dx, 24:32]
            out.append(
                pltpu.make_async_remote_copy(
                    src_ref=src,
                    dst_ref=dst,
                    send_sem=send_sem.at[m],
                    recv_sem=recv_sem.at[s, o],
                    device_id=device(d),
                    device_id_type=MESH,
                )
            )
        return out

    def each(s, nc, which, act):
        for t in transfers(s, nc, which):
            act(t)

    def start(s, nc, which):
        def go(dx):
            return lambda: each(s, nc, lambda d: d[0] == dx and which(d), lambda t: t.start())

        if any(d[0] and which(d) for d in PARTNERS):
            by_side(go(-1), go(0), go(1))
        else:
            go(0)()

    def wait_sent(s, nc):
        by_side(
            lambda: each(s, nc, lambda d: d[0] == -1, lambda t: t.wait_send()),
            lambda: each(s, nc, lambda d: d[0] == 0, lambda t: t.wait_send()),
            lambda: each(s, nc, lambda d: d[0] == 1, lambda t: t.wait_send()),
        )

    def wait_beside(s, nc):
        each(s, nc, lambda d: d == (0, 0, 1), lambda t: t.wait_recv())

    def wait_rows(s, nc):
        each(s, nc, lambda d: d[0] == 0 and d[1], lambda t: t.wait_recv())

    def wait_far(s, nc, which):
        pl.when(has_left)(lambda: each(s, nc, lambda d: d[0] == 1 and which(d), lambda t: t.wait_recv()))
        pl.when(has_right)(lambda: each(s, nc, lambda d: d[0] == -1 and which(d), lambda t: t.wait_recv()))

    def pack_corners(s, nc):
        for c in range(nc):
            csend[0, c : c + 1, :] = grid[s, c, 2, 8:9, :]
            csend[1, c : c + 1, :] = grid[s, c, 2, 23:24, :]
            csend[2, c : c + 1, :] = grid[s, c, 9, 8:9, :]
            csend[3, c : c + 1, :] = grid[s, c, 9, 23:24, :]

    def pack_columns(s, planes, nc, fresh):
        for t in range(2):
            packed = None if fresh else qsend[8 * t : 8 * t + 8, :]
            for c in range(nc):
                for p in planes:
                    k = c * 8 + p
                    tile = grid[s, c, p + 2, 8 + 8 * t : 16 + 8 * t, :]
                    moved = pltpu.roll(tile, 2 * k, 1) if k else tile
                    packed = moved if packed is None else jnp.where(pair == k, moved, packed)
            qsend[8 * t : 8 * t + 8, :] = packed

    def pack_rows(s, planes, nc):
        for c in range(nc):
            for p in planes:
                at = 2 * (p % 4)
                zsend[0, c, p // 4, at : at + 2, :] = grid[s, c, p + 2, 8:10, :]
                zsend[1, c, p // 4, at : at + 2, :] = grid[s, c, p + 2, 22:24, :]

    SHIFTS = ((0, 127), (1, 1), (2, 126), (3, 2))

    def turn_own(s, planes, nc, far):
        for c in range(nc):
            for p in planes:
                for r in (1, 2):
                    rows = slice(8 * r, 8 * r + 8)
                    tile = grid[s, c, p + 2, rows, :]
                    for n, by in SHIFTS[:2] if far else SHIFTS:
                        turned[n, c, p + 2, rows, :] = pltpu.roll(tile, by, 1)

    def turn_rows(s, planes, nc):
        for c in range(nc):
            for p in planes:
                ends = jnp.where(row < 4, grid[s, c, p + 2, 24:32, :], grid[s, c, p + 2, 0:8, :])
                for n, by in SHIFTS[:2]:
                    moved = pltpu.roll(ends, by, 1)
                    turned[n, c, p + 2, 0:8, :] = moved
                    turned[n, c, p + 2, 24:32, :] = moved

    def close_seam(s, planes, nc, tiles=(0, 1, 2, 3)):
        for c in range(nc):
            for p in planes:
                slot, plane = (1, p) if 0 <= p < 8 else ((0, 7) if p < 0 else (2, 0))
                k = c * 8 + plane

                def other(tile, step):
                    return pltpu.roll(tile, lax.rem(swing[step] + (256 - 2 * k), 128), 1)

                if 0 in tiles:
                    ends = jnp.where(row < 4, qrecv[s, slot, 24:32, :], qrecv[s, slot, 0:8, :])
                    ends = other(ends, 1)
                for r in tiles:
                    rows = slice(8 * r, 8 * r + 8)
                    inner_rows = r in (1, 2)
                    here = turned[gy, c, p + 2, rows, :]
                    there = other(qrecv[s, slot, rows, :], 1) if inner_rows else ends
                    turned[gy, c, p + 2, rows, :] = jnp.where(from_other[1], there, here)
                    if inner_rows and slot == 1:
                        here = turned[2 + gy, c, p + 2, rows, :]
                        there = other(qrecv[s, slot, rows, :], 2)
                        turned[2 + gy, c, p + 2, rows, :] = jnp.where(from_other[2], there, here)

    def spread_near(s, nc):
        for c in range(nc):
            for p in range(8):
                at = 2 * (p % 4)
                grid[s, c, p + 2, 6:8, :] = zrecv[s, 0, c, p // 4, at : at + 2, :]
                grid[s, c, p + 2, 24:26, :] = zrecv[s, 1, c, p // 4, at : at + 2, :]
        turn_rows(s, range(8), nc)
        close_seam(s, range(8), nc, (0, 3))

    def spread_planes(s, nc):
        turn_own(s, (-1, 8), nc, True)
        close_seam(s, (-1, 8), nc, (1, 2))

    def spread_far(s, nc):
        for c in range(nc):
            grid[s, c, 1, 7:8, :] = crecv[s, 0, c : c + 1, :]
            grid[s, c, 1, 24:25, :] = crecv[s, 1, c : c + 1, :]
            grid[s, c, 10, 7:8, :] = crecv[s, 2, c : c + 1, :]
            grid[s, c, 10, 24:25, :] = crecv[s, 3, c : c + 1, :]
        turn_rows(s, (-1, 8), nc)
        close_seam(s, (-1, 8), nc, (0, 3))

    def needs_near(e, t):
        return 2 if (t == 0 and e[2] < 0) or (t == 1 and e[2] > 0) else 1 if e[1] else 0

    def bonds(s, p, dirs, first, onto, part, x_inside=None):
        for t in range(2):
            chosen = [e for e in dirs if needs_near(e, t) in part]
            mine = slice(8 * t, 8 * t + 8)
            base = slice(8 + 8 * t, 16 + 8 * t)
            centre = [grid[s, c, p + 2, base, :] for c in range(3)]
            moved = {}
            for c in range(3):
                for e in range(-2, 3):
                    moved[c, e] = centre[c] - float(e) if e else centre[c]
            if first:
                own_c, own_q = grid[s, 3, p + 2, base, :], grid[s, 4, p + 2, base, :]
            total = [acc[c, p, mine, :] for c in range(3)] if onto else [None] * 3
            for e in chosen:
                ex, ey, ez = e
                length = math.sqrt(ex * ex + ey * ey + ez * ez)
                rows = slice(8 + 8 * t + ez, 16 + 8 * t + ez)
                field = {1: 0, -1: 1, 2: 2, -2: 3}.get(ey)

                def near(c):
                    if field is None:
                        return grid[s, c, p + 2 + ex, rows, :]
                    return turned[field, c, p + 2 + ex, rows, :]

                n = WHERE[e]
                if first:
                    a = (own_c + near(3)) * (0.5 / (length * length))
                    if x_inside is not None:
                        a = a * x_inside
                    if ey:
                        here = lane + (128 * gy + ey)
                        a = jnp.where((here >= 0) & (here < 256), a, 0.0)
                    if (t == 0 and ez < 0) or (t == 1 and ez > 0):
                        here = row + (16 * gz + 8 * t + ez)
                        a = jnp.where((here >= 0) & (here < 16 * nz), a, 0.0)
                    b = (-2.0 / (length * math.log(2.0))) / (own_q + near(4))
                    coef[n, 0, p, mine, :] = a
                    coef[n, 1, p, mine, :] = b
                else:
                    a = coef[n, 0, p, mine, :]
                    b = coef[n, 1, p, mine, :]
                sx = near(0) - moved[0, ex]
                sy = near(1) - moved[1, ey]
                sz = near(2) - moved[2, ez]
                square = jnp.maximum(sx * sx + sy * sy + sz * sz, TINY)
                inverse = lax.rsqrt(square)
                over = square * inverse - length
                pull = (a * over) * inverse * jnp.exp2(b * jnp.abs(over))
                for c, way in enumerate((sx, sy, sz)):
                    add = pull * way
                    total[c] = add if total[c] is None else total[c] + add
            for c in range(3):
                acc[c, p, mine, :] = total[c]

    inner = {
        0: [e for e in DIRS if e[0] >= 0],
        1: [e for e in DIRS if e[0] >= -1],
        6: [e for e in DIRS if e[0] <= 1],
        7: [e for e in DIRS if e[0] <= 0],
    }

    def near_bonds(s, first, part):
        for p in (0, 1, 6, 7):
            bonds(s, p, inner[p], first, part > 0, (part,))

        def middle(p, carry):
            bonds(s, p, DIRS, first, part > 0, (part,))
            return carry

        lax.fori_loop(2, 6, middle, 0)

    def far_bonds(s, planes, first, part):
        for p in planes:
            inside = None
            if first:
                inside = jnp.where(has_left if p < 2 else has_right, 1.0, 0.0)
            bonds(s, p, [e for e in DIRS if e not in inner[p]], first, True, part, inside)

    def advance(s, planes, weight):
        for p in planes:
            for c in range(3):
                new = free[p] * (speed[c, p] + weight * acc[c, p])
                speed[c, p] = new
                grid[1 - s, c, p + 2, 8:24, :] = grid[s, c, p + 2, 8:24, :] + DT * new

    def send(s, nc, late):
        pack_corners(s, nc)
        start(s, nc, lambda d: d[0] and d[1] and not d[2])
        pack_columns(s, late, nc, False)
        start(s, nc, lambda d: d[0] and d[2])
        start(s, nc, lambda d: not d[0] and d[2])
        start(s, nc, lambda d: d[0] and not d[1] and not d[2])
        pack_rows(s, late, nc)
        start(s, nc, lambda d: not d[0] and not d[2])

    def run(s, nc, first, weight, go_on):
        turn_own(s, range(8), nc, False)
        near_bonds(s, first, 0)
        wait_beside(s, nc)
        close_seam(s, range(8), nc, (1, 2))
        near_bonds(s, first, 1)
        wait_rows(s, nc)
        spread_near(s, nc)
        near_bonds(s, first, 2)
        advance(s, range(2, 6), weight)
        wait_sent(s, nc)
        pack_columns(1 - s, range(2, 6), 3, True)
        pack_rows(1 - s, range(2, 6), 3)
        wait_far(s, nc, lambda d: not d[1])
        spread_planes(s, nc)
        far_bonds(s, (1, 6, 0, 7), first, (0, 1))
        advance(s, (1, 6), weight)
        pack_columns(1 - s, (1, 6), 3, False)
        pack_rows(1 - s, (1, 6), 3)
        wait_far(s, nc, lambda d: d[1])
        spread_far(s, nc)
        far_bonds(s, (0, 7), first, (2,))
        advance(s, (0, 7), weight)
        go_on(lambda: send(1 - s, 3, (0, 7)))

    loads[4].wait()
    loads[5].wait()
    loads[0].wait()
    for p in range(8):
        kind = cls[p]
        c_of = jnp.where(kind == 1, table_c[1], table_c[0])
        c_of = jnp.where(kind == 2, table_c[2], c_of)
        c_of = jnp.where(kind == 3, table_c[3], c_of)
        q_of = jnp.where(kind == 1, table_q[1], table_q[0])
        q_of = jnp.where(kind == 2, table_q[2], q_of)
        q_of = jnp.where(kind == 3, table_q[3], q_of)
        grid[0, 3, p + 2, 8:24, :] = c_of
        grid[0, 4, p + 2, 8:24, :] = q_of
    loads[1].wait()
    pack_columns(0, range(2, 6), 5, True)
    pack_rows(0, range(2, 6), 5)
    pl.semaphore_wait(barrier, 5 + jnp.where(has_left, 6, 0) + jnp.where(has_right, 6, 0))
    send(0, 5, (0, 1, 6, 7))
    loads[2].wait()
    loads[3].wait()
    for p in range(8):
        free[p] = 1.0 - clm[p].astype(jnp.float32)

    run(0, 5, True, HALF, lambda f: f())

    stores = [
        pltpu.make_async_copy(grid.at[STEPS % 2, 0:3, 2:10, 8:24], u_out, local_sem.at[1]),
        pltpu.make_async_copy(speed, v_out, local_sem.at[2]),
    ]

    def step(k, carry):
        weight = jnp.where(k == STEPS, HALF, DT)

        def go_on(f):
            @pl.when(k < STEPS)
            def _():
                f()

        @pl.when(k == STEPS)
        def _():
            stores[0].start()

        run(lax.rem(k, 2), 3, False, weight, go_on)
        return carry

    lax.fori_loop(1, STEPS + 1, step, 0)

    stores[1].start()
    for c in stores:
        c.wait()


def put_out(u_from, v_from, u_to, v_to, sems):
    moves = [
        pltpu.make_async_copy(u_from, u_to, sems.at[0]),
        pltpu.make_async_copy(v_from, v_to, sems.at[1]),
    ]
    for c in moves:
        c.start()
    for c in moves:
        c.wait()


def local(displacement, velocity, classes, clamped, stiffness, softening):
    block = displacement.shape
    f32 = jnp.float32
    anywhere = pl.BlockSpec(memory_space=pl.ANY)
    outside = pl.BlockSpec(memory_space=pltpu.HBM)
    results = pl.pallas_call(
        kernel,
        out_shape=[jax.ShapeDtypeStruct(block, f32)] * 2,
        in_specs=[outside] * 6,
        out_specs=[anywhere] * 2,
        scratch_shapes=[
            pltpu.SMEM((4,), f32),
            pltpu.SMEM((4,), f32),
            pltpu.VMEM((2, 5, 12, 32, 128), f32),
            pltpu.VMEM((4, 5, 12, 32, 128), f32),
            pltpu.VMEM((3, 8, 16, 128), f32),
            pltpu.VMEM((8, 16, 128), jnp.int32),
            pltpu.VMEM((8, 16, 128), jnp.int32),
            pltpu.VMEM((8, 16, 128), f32),
            pltpu.VMEM((3, 8, 16, 128), f32),
            pltpu.VMEM((len(DIRS), 2, 8, 16, 128), f32),
            pltpu.VMEM((2, 5, 2, 8, 128), f32),
            pltpu.VMEM((2, 2, 5, 2, 8, 128), f32),
            pltpu.VMEM((4, 8, 128), f32),
            pltpu.VMEM((2, 4, 8, 128), f32),
            pltpu.VMEM((16, 128), f32),
            pltpu.VMEM((2, 3, 32, 128), f32),
            pltpu.SemaphoreType.DMA((6,)),
            pltpu.SemaphoreType.DMA((NP,)),
            pltpu.SemaphoreType.DMA((2, NP)),
        ],
        compiler_params=pltpu.CompilerParams(collective_id=0, has_side_effects=True, vmem_limit_bytes=15 << 20),
    )(*(pltpu.with_memory_space_constraint(x, pltpu.HBM) for x in (stiffness, softening, displacement, velocity, classes, clamped)))
    return pl.pallas_call(
        put_out,
        out_shape=[jax.ShapeDtypeStruct(block, f32)] * 2,
        in_specs=[anywhere] * 2,
        out_specs=[anywhere] * 2,
        scratch_shapes=[pltpu.SemaphoreType.DMA((2,))],
        compiler_params=pltpu.CompilerParams(vmem_limit_bytes=1 << 20),
    )(*results)


def solution(mesh):
    return jax.shard_map(
        local,
        mesh=mesh,
        in_specs=(
            P(None, "gx", "gz", "gy"),
            P(None, "gx", "gz", "gy"),
            P("gx", "gz", "gy"),
            P("gx", "gz", "gy"),
            P(),
            P(),
        ),
        out_specs=(P(None, "gx", "gz", "gy"), P(None, "gx", "gz", "gy")),
        check_vma=False,
    )
```

```python
import math

import jax
import jax.numpy as jnp
from jax import lax
from jax.experimental import pallas as pl
from jax.experimental.pallas import tpu as pltpu
from jax.sharding import PartitionSpec as P

STEPS = 4
DT = 0.2
HALF = 0.1
MESH = pl.DeviceIdType.MESH

DIRS = [
    (ex, ey, ez)
    for ex in range(-2, 3)
    for ey in range(-2, 3)
    for ez in range(-2, 3)
    if 0 < ex * ex + ey * ey + ez * ez <= 4
]
WHERE = {e: n for n, e in enumerate(DIRS)}
PARTNERS = [
    (dx, dz, dy)
    for dx in (-1, 0, 1)
    for dz in (-1, 0, 1)
    for dy in (0, 1)
    if (dx, dz, dy) != (0, 0, 0)
]
SLOT = {d: n for n, d in enumerate(PARTNERS)}
NP = len(PARTNERS)
TINY = 1e-30


def opposite(d):
    return (-d[0], -d[1], d[2])


def kernel(
    table_c_in, table_q_in, u_in, v_in, class_in, clamp_in,
    u_out, speed,
    table_c, table_q, grid, turned, cls, clm, free, acc, coef,
    zsend, zrecv, csend, crecv, qsend, qrecv,
    local_sem, send_sem, recv_sem,
):
    gx, gy, gz = lax.axis_index("gx"), lax.axis_index("gy"), lax.axis_index("gz")
    nx, nz = lax.axis_size("gx"), lax.axis_size("gz")

    def device(d):
        return {
            "gx": lax.rem(gx + (d[0] + nx), nx),
            "gz": lax.rem(gz + (d[1] + nz), nz),
            "gy": 1 - gy if d[2] else gy,
        }

    has_left, has_right = gx > 0, gx < nx - 1

    def by_side(left, beside, right):
        pl.when(has_left)(left)
        beside()
        pl.when(has_right)(right)

    barrier = pltpu.get_barrier_semaphore()

    def greet(dx):
        def go():
            for d in PARTNERS:
                if d[0] == dx:
                    pl.semaphore_signal(barrier, inc=1, device_id=device(d), device_id_type=MESH)

        return go

    by_side(greet(-1), greet(0), greet(1))

    zero = jnp.zeros((8, 128), jnp.float32)

    def clear(planes, slot, corners):
        def go():
            for par in range(2):
                for r in range(4):
                    rows = slice(8 * r, 8 * r + 8)
                    for c in range(5):
                        for plane in planes:
                            grid[par, c, plane, rows, :] = zero
                    qrecv[par, slot, rows, :] = zero
                for q in corners:
                    crecv[par, q] = zero

        return go

    pl.when(jnp.logical_not(has_left))(clear((0, 1), 0, (0, 1)))
    pl.when(jnp.logical_not(has_right))(clear((10, 11), 2, (2, 3)))

    loads = [
        pltpu.make_async_copy(class_in, cls, local_sem.at[0]),
        pltpu.make_async_copy(u_in, grid.at[0, 0:3, 2:10, 8:24], local_sem.at[1]),
        pltpu.make_async_copy(v_in, speed, local_sem.at[2]),
        pltpu.make_async_copy(clamp_in, clm, local_sem.at[3]),
        pltpu.make_async_copy(table_c_in, table_c, local_sem.at[4]),
        pltpu.make_async_copy(table_q_in, table_q, local_sem.at[5]),
    ]
    for c in loads:
        c.start()

    lane = lax.broadcasted_iota(jnp.int32, (8, 128), 1)
    row = lax.broadcasted_iota(jnp.int32, (8, 128), 0)
    upper = gy == 1
    pair = lax.rem(lane - jnp.where(upper, 0, 126) + 128, 128) // 2
    from_other = {
        1: lane == jnp.where(upper, 0, 127),
        2: (lane >= jnp.where(upper, 0, 126)) & (lane < jnp.where(upper, 2, 128)),
    }
    swing = {1: jnp.where(upper, 1, 127), 2: jnp.where(upper, 2, 126)}

    def transfers(s, nc, which=lambda d: True):
        out = []
        for d in PARTNERS:
            if not which(d):
                continue
            dx, dz, dy = d
            m = SLOT[d]
            o = SLOT[opposite(d)]
            if d == (-1, 0, 0):
                src, dst = grid.at[s, 0:nc, 2:4, 8:24], grid.at[s, 0:nc, 10:12, 8:24]
            elif d == (1, 0, 0):
                src, dst = grid.at[s, 0:nc, 8:10, 8:24], grid.at[s, 0:nc, 0:2, 8:24]
            elif dy == 0 and dx == 0:
                side = 0 if dz < 0 else 1
                src, dst = zsend.at[side, 0:nc], zrecv.at[s, 1 - side, 0:nc]
            elif dy == 0:
                q = (0 if dx < 0 else 2) + (0 if dz < 0 else 1)
                src, dst = csend.at[q], crecv.at[s, 3 - q]
            else:
                if dz == 0:
                    src, dst = qsend.at[...], qrecv.at[s, 1 - dx, 8:24]
                elif dz > 0:
                    src, dst = qsend.at[8:16], qrecv.at[s, 1 - dx, 0:8]
                else:
                    src, dst = qsend.at[0:8], qrecv.at[s, 1 - dx, 24:32]
            out.append(
                pltpu.make_async_remote_copy(
                    src_ref=src,
                    dst_ref=dst,
                    send_sem=send_sem.at[m],
                    recv_sem=recv_sem.at[s, o],
                    device_id=device(d),
                    device_id_type=MESH,
                )
            )
        return out

    def each(s, nc, which, act):
        for t in transfers(s, nc, which):
            act(t)

    def start(s, nc, which):
        def go(dx):
            return lambda: each(s, nc, lambda d: d[0] == dx and which(d), lambda t: t.start())

        if any(d[0] and which(d) for d in PARTNERS):
            by_side(go(-1), go(0), go(1))
        else:
            go(0)()

    def wait_sent(s, nc):
        by_side(
            lambda: each(s, nc, lambda d: d[0] == -1, lambda t: t.wait_send()),
            lambda: each(s, nc, lambda d: d[0] == 0, lambda t: t.wait_send()),
            lambda: each(s, nc, lambda d: d[0] == 1, lambda t: t.wait_send()),
        )

    def wait_beside(s, nc):
        each(s, nc, lambda d: d == (0, 0, 1), lambda t: t.wait_recv())

    def wait_rows(s, nc):
        each(s, nc, lambda d: d[0] == 0 and d[1], lambda t: t.wait_recv())

    def wait_far(s, nc, which):
        pl.when(has_left)(lambda: each(s, nc, lambda d: d[0] == 1 and which(d), lambda t: t.wait_recv()))
        pl.when(has_right)(lambda: each(s, nc, lambda d: d[0] == -1 and which(d), lambda t: t.wait_recv()))

    def pack_corners(s, nc):
        for c in range(nc):
            csend[0, c : c + 1, :] = grid[s, c, 2, 8:9, :]
            csend[1, c : c + 1, :] = grid[s, c, 2, 23:24, :]
            csend[2, c : c + 1, :] = grid[s, c, 9, 8:9, :]
            csend[3, c : c + 1, :] = grid[s, c, 9, 23:24, :]

    def pack_columns(s, planes, nc, fresh):
        for t in range(2):
            packed = None if fresh else qsend[8 * t : 8 * t + 8, :]
            for c in range(nc):
                for p in planes:
                    k = c * 8 + p
                    tile = grid[s, c, p + 2, 8 + 8 * t : 16 + 8 * t, :]
                    moved = pltpu.roll(tile, 2 * k, 1) if k else tile
                    packed = moved if packed is None else jnp.where(pair == k, moved, packed)
            qsend[8 * t : 8 * t + 8, :] = packed

    def pack_rows(s, planes, nc):
        for c in range(nc):
            for p in planes:
                at = 2 * (p % 4)
                zsend[0, c, p // 4, at : at + 2, :] = grid[s, c, p + 2, 8:10, :]
                zsend[1, c, p // 4, at : at + 2, :] = grid[s, c, p + 2, 22:24, :]

    SHIFTS = ((0, 127), (1, 1), (2, 126), (3, 2))

    def turn_own(s, planes, nc, far):
        for c in range(nc):
            for p in planes:
                for r in (1, 2):
                    rows = slice(8 * r, 8 * r + 8)
                    tile = grid[s, c, p + 2, rows, :]
                    for n, by in SHIFTS[:2] if far else SHIFTS:
                        turned[n, c, p + 2, rows, :] = pltpu.roll(tile, by, 1)

    def turn_rows(s, planes, nc):
        for c in range(nc):
            for p in planes:
                ends = jnp.where(row < 4, grid[s, c, p + 2, 24:32, :], grid[s, c, p + 2, 0:8, :])
                for n, by in SHIFTS[:2]:
                    moved = pltpu.roll(ends, by, 1)
                    turned[n, c, p + 2, 0:8, :] = moved
                    turned[n, c, p + 2, 24:32, :] = moved

    def close_seam(s, planes, nc, tiles=(0, 1, 2, 3)):
        for c in range(nc):
            for p in planes:
                slot, plane = (1, p) if 0 <= p < 8 else ((0, 7) if p < 0 else (2, 0))
                k = c * 8 + plane

                def other(tile, step):
                    return pltpu.roll(tile, lax.rem(swing[step] + (256 - 2 * k), 128), 1)

                if 0 in tiles:
                    ends = jnp.where(row < 4, qrecv[s, slot, 24:32, :], qrecv[s, slot, 0:8, :])
                    ends = other(ends, 1)
                for r in tiles:
                    rows = slice(8 * r, 8 * r + 8)
                    inner_rows = r in (1, 2)
                    here = turned[gy, c, p + 2, rows, :]
                    there = other(qrecv[s, slot, rows, :], 1) if inner_rows else ends
                    turned[gy, c, p + 2, rows, :] = jnp.where(from_other[1], there, here)
                    if inner_rows and slot == 1:
                        here = turned[2 + gy, c, p + 2, rows, :]
                        there = other(qrecv[s, slot, rows, :], 2)
                        turned[2 + gy, c, p + 2, rows, :] = jnp.where(from_other[2], there, here)

    def spread_near(s, nc):
        for c in range(nc):
            for p in range(8):
                at = 2 * (p % 4)
                grid[s, c, p + 2, 6:8, :] = zrecv[s, 0, c, p // 4, at : at + 2, :]
                grid[s, c, p + 2, 24:26, :] = zrecv[s, 1, c, p // 4, at : at + 2, :]
        turn_rows(s, range(8), nc)
        close_seam(s, range(8), nc, (0, 3))

    def spread_planes(s, nc):
        turn_own(s, (-1, 8), nc, True)
        close_seam(s, (-1, 8), nc, (1, 2))

    def spread_far(s, nc):
        for c in range(nc):
            grid[s, c, 1, 7:8, :] = crecv[s, 0, c : c + 1, :]
            grid[s, c, 1, 24:25, :] = crecv[s, 1, c : c + 1, :]
            grid[s, c, 10, 7:8, :] = crecv[s, 2, c : c + 1, :]
            grid[s, c, 10, 24:25, :] = crecv[s, 3, c : c + 1, :]
        turn_rows(s, (-1, 8), nc)
        close_seam(s, (-1, 8), nc, (0, 3))

    def needs_near(e, t):
        return 2 if (t == 0 and e[2] < 0) or (t == 1 and e[2] > 0) else 1 if e[1] else 0

    def bonds(s, p, dirs, first, onto, part, x_inside=None):
        for t in range(2):
            chosen = [e for e in dirs if needs_near(e, t) in part]
            mine = slice(8 * t, 8 * t + 8)
            base = slice(8 + 8 * t, 16 + 8 * t)
            centre = [grid[s, c, p + 2, base, :] for c in range(3)]
            moved = {}
            for c in range(3):
                for e in range(-2, 3):
                    moved[c, e] = centre[c] - float(e) if e else centre[c]
            if first:
                own_c, own_q = grid[s, 3, p + 2, base, :], grid[s, 4, p + 2, base, :]
            total = [acc[c, p, mine, :] for c in range(3)] if onto else [None] * 3
            for e in chosen:
                ex, ey, ez = e
                length = math.sqrt(ex * ex + ey * ey + ez * ez)
                rows = slice(8 + 8 * t + ez, 16 + 8 * t + ez)
                field = {1: 0, -1: 1, 2: 2, -2: 3}.get(ey)

                def near(c):
                    if field is None:
                        return grid[s, c, p + 2 + ex, rows, :]
                    return turned[field, c, p + 2 + ex, rows, :]

                n = WHERE[e]
                if first:
                    a = (own_c + near(3)) * (0.5 / (length * length))
                    if x_inside is not None:
                        a = a * x_inside
                    if ey:
                        here = lane + (128 * gy + ey)
                        a = jnp.where((here >= 0) & (here < 256), a, 0.0)
                    if (t == 0 and ez < 0) or (t == 1 and ez > 0):
                        here = row + (16 * gz + 8 * t + ez)
                        a = jnp.where((here >= 0) & (here < 16 * nz), a, 0.0)
                    b = (-2.0 / (length * math.log(2.0))) / (own_q + near(4))
                    coef[n, 0, p, mine, :] = a
                    coef[n, 1, p, mine, :] = b
                else:
                    a = coef[n, 0, p, mine, :]
                    b = coef[n, 1, p, mine, :]
                sx = near(0) - moved[0, ex]
                sy = near(1) - moved[1, ey]
                sz = near(2) - moved[2, ez]
                square = jnp.maximum(sx * sx + sy * sy + sz * sz, TINY)
                inverse = lax.rsqrt(square)
                over = square * inverse - length
                pull = (a * over) * inverse * jnp.exp2(b * jnp.abs(over))
                for c, way in enumerate((sx, sy, sz)):
                    add = pull * way
                    total[c] = add if total[c] is None else total[c] + add
            for c in range(3):
                acc[c, p, mine, :] = total[c]

    inner = {
        0: [e for e in DIRS if e[0] >= 0],
        1: [e for e in DIRS if e[0] >= -1],
        6: [e for e in DIRS if e[0] <= 1],
        7: [e for e in DIRS if e[0] <= 0],
    }

    def near_bonds(s, first, part):
        for p in (0, 1, 6, 7):
            bonds(s, p, inner[p], first, part > 0, (part,))

        def middle(p, carry):
            bonds(s, p, DIRS, first, part > 0, (part,))
            return carry

        lax.fori_loop(2, 6, middle, 0)

    def far_bonds(s, planes, first, part):
        for p in planes:
            inside = None
            if first:
                inside = jnp.where(has_left if p < 2 else has_right, 1.0, 0.0)
            bonds(s, p, [e for e in DIRS if e not in inner[p]], first, True, part, inside)

    def advance(s, planes, weight):
        for p in planes:
            for c in range(3):
                new = free[p] * (speed[c, p] + weight * acc[c, p])
                speed[c, p] = new
                grid[1 - s, c, p + 2, 8:24, :] = grid[s, c, p + 2, 8:24, :] + DT * new

    def send(s, nc, late):
        pack_corners(s, nc)
        start(s, nc, lambda d: d[0] and d[1] and not d[2])
        pack_columns(s, late, nc, False)
        start(s, nc, lambda d: d[0] and d[2])
        start(s, nc, lambda d: not d[0] and d[2])
        start(s, nc, lambda d: d[0] and not d[1] and not d[2])
        pack_rows(s, late, nc)
        start(s, nc, lambda d: not d[0] and not d[2])

    def run(s, nc, first, weight, go_on):
        turn_own(s, range(8), nc, False)
        near_bonds(s, first, 0)
        wait_beside(s, nc)
        close_seam(s, range(8), nc, (1, 2))
        near_bonds(s, first, 1)
        wait_rows(s, nc)
        spread_near(s, nc)
        near_bonds(s, first, 2)
        advance(s, range(2, 6), weight)
        wait_sent(s, nc)
        pack_columns(1 - s, range(2, 6), 3, True)
        pack_rows(1 - s, range(2, 6), 3)
        wait_far(s, nc, lambda d: not d[1])
        spread_planes(s, nc)
        far_bonds(s, (1, 6, 0, 7), first, (0, 1))
        advance(s, (1, 6), weight)
        pack_columns(1 - s, (1, 6), 3, False)
        pack_rows(1 - s, (1, 6), 3)
        wait_far(s, nc, lambda d: d[1])
        spread_far(s, nc)
        far_bonds(s, (0, 7), first, (2,))
        advance(s, (0, 7), weight)
        go_on(lambda: send(1 - s, 3, (0, 7)))

    loads[4].wait()
    loads[5].wait()
    loads[0].wait()
    for p in range(8):
        kind = cls[p]
        c_of = jnp.where(kind == 1, table_c[1], table_c[0])
        c_of = jnp.where(kind == 2, table_c[2], c_of)
        c_of = jnp.where(kind == 3, table_c[3], c_of)
        q_of = jnp.where(kind == 1, table_q[1], table_q[0])
        q_of = jnp.where(kind == 2, table_q[2], q_of)
        q_of = jnp.where(kind == 3, table_q[3], q_of)
        grid[0, 3, p + 2, 8:24, :] = c_of
        grid[0, 4, p + 2, 8:24, :] = q_of
    loads[1].wait()
    pack_columns(0, range(2, 6), 5, True)
    pack_rows(0, range(2, 6), 5)
    pl.semaphore_wait(barrier, 5 + jnp.where(has_left, 6, 0) + jnp.where(has_right, 6, 0))
    send(0, 5, (0, 1, 6, 7))
    loads[2].wait()
    loads[3].wait()
    for p in range(8):
        free[p] = 1.0 - clm[p].astype(jnp.float32)

    run(0, 5, True, HALF, lambda f: f())

    stores = [
        pltpu.make_async_copy(grid.at[STEPS % 2, 0:3, 2:10, 8:24], u_out, local_sem.at[1]),
    ]

    def step(k, carry):
        weight = jnp.where(k == STEPS, HALF, DT)

        def go_on(f):
            @pl.when(k < STEPS)
            def _():
                f()

        @pl.when(k == STEPS)
        def _():
            stores[0].start()

        run(lax.rem(k, 2), 3, False, weight, go_on)
        return carry

    lax.fori_loop(1, STEPS + 1, step, 0)

    for c in stores:
        c.wait()


def put_out(u_from, v_from, u_to, v_to, sems):
    moves = [
        pltpu.make_async_copy(u_from, u_to, sems.at[0]),
        pltpu.make_async_copy(v_from, v_to, sems.at[1]),
    ]
    for c in moves:
        c.start()
    for c in moves:
        c.wait()


def local(displacement, velocity, classes, clamped, stiffness, softening):
    block = displacement.shape
    f32 = jnp.float32
    anywhere = pl.BlockSpec(memory_space=pl.ANY)
    outside = pl.BlockSpec(memory_space=pltpu.HBM)
    results = pl.pallas_call(
        kernel,
        out_shape=[jax.ShapeDtypeStruct(block, f32)] * 2,
        in_specs=[outside] * 6,
        out_specs=[anywhere, pl.BlockSpec(memory_space=pltpu.VMEM)],
        scratch_shapes=[
            pltpu.SMEM((4,), f32),
            pltpu.SMEM((4,), f32),
            pltpu.VMEM((2, 5, 12, 32, 128), f32),
            pltpu.VMEM((4, 5, 12, 32, 128), f32),
            pltpu.VMEM((8, 16, 128), jnp.int32),
            pltpu.VMEM((8, 16, 128), jnp.int32),
            pltpu.VMEM((8, 16, 128), f32),
            pltpu.VMEM((3, 8, 16, 128), f32),
            pltpu.VMEM((len(DIRS), 2, 8, 16, 128), f32),
            pltpu.VMEM((2, 5, 2, 8, 128), f32),
            pltpu.VMEM((2, 2, 5, 2, 8, 128), f32),
            pltpu.VMEM((4, 8, 128), f32),
            pltpu.VMEM((2, 4, 8, 128), f32),
            pltpu.VMEM((16, 128), f32),
            pltpu.VMEM((2, 3, 32, 128), f32),
            pltpu.SemaphoreType.DMA((6,)),
            pltpu.SemaphoreType.DMA((NP,)),
            pltpu.SemaphoreType.DMA((2, NP)),
        ],
        compiler_params=pltpu.CompilerParams(collective_id=0, has_side_effects=True, vmem_limit_bytes=15 << 20),
    )(*(pltpu.with_memory_space_constraint(x, pltpu.HBM) for x in (stiffness, softening, displacement, velocity, classes, clamped)))
    return pl.pallas_call(
        put_out,
        out_shape=[jax.ShapeDtypeStruct(block, f32)] * 2,
        in_specs=[anywhere] * 2,
        out_specs=[anywhere] * 2,
        scratch_shapes=[pltpu.SemaphoreType.DMA((2,))],
        compiler_params=pltpu.CompilerParams(vmem_limit_bytes=1 << 20),
    )(*results)


def solution(mesh):
    return jax.shard_map(
        local,
        mesh=mesh,
        in_specs=(
            P(None, "gx", "gz", "gy"),
            P(None, "gx", "gz", "gy"),
            P("gx", "gz", "gy"),
            P("gx", "gz", "gy"),
            P(),
            P(),
        ),
        out_specs=(P(None, "gx", "gz", "gy"), P(None, "gx", "gz", "gy")),
        check_vma=False,
    )
```
